32 devices in a mesh: dp: 16 (over z, x, core), tensor: 2 (over y).
Axes of the slice: x: 2, y: 2, z: 4, core: 2. Of those that a mesh axis runs over, the one named last changes fastest.
Arguments:
- tokens: bfloat16 [32, 512, 1024], P('dp', 'tensor')
- clip_count: int32 [16], P('dp'), may hold values from 1 to 2, as said below
- first_norm_gain: bfloat16 [1024], replicated, may hold values from 0.5 to 1.5
- first_norm_shift: bfloat16 [1024], replicated, may hold values from -1.5 to 1.5
- first_up_weight: bfloat16 [1024, 4096], P(None, 'tensor'), may hold values from -0.1875 to 0.1875
- first_up_bias: bfloat16 [4096], P('tensor'), may hold values from -1.5 to 1.5
- first_down_weight: bfloat16 [4096, 1024], P('tensor'), may hold values from -0.1875 to 0.1875
- first_down_bias: bfloat16 [1024], replicated, may hold values from -1.5 to 1.5
- attend_norm_gain: bfloat16 [1024], replicated, may hold values from 0.5 to 1.5
- attend_norm_shift: bfloat16 [1024], replicated, may hold values from -1.5 to 1.5
- query_weight: bfloat16 [1024, 1024], P(None, 'tensor'), may hold values from -0.1875 to 0.1875
- query_bias: bfloat16 [1024], P('tensor'), may hold values from -1.5 to 1.5
- key_weight: bfloat16 [1024, 1024], P(None, 'tensor'), may hold values from -0.1875 to 0.1875
- value_weight: bfloat16 [1024, 1024], P(None, 'tensor'), may hold values from -0.1875 to 0.1875
- value_bias: bfloat16 [1024], P('tensor'), may hold values from -1.5 to 1.5
- output_weight: bfloat16 [1024, 1024], P('tensor'), may hold values from -1.5 to 1.5
- output_bias: bfloat16 [1024], replicated, may hold values from -1.5 to 1.5
- relative_table: bfloat16 [73, 64], replicated, may hold values from -5 to 5
- convolve_norm_gain: bfloat16 [1024], replicated, may hold values from 0.5 to 1.5
- convolve_norm_shift: bfloat16 [1024], replicated, may hold values from -1.5 to 1.5
- pointwise_in: bfloat16 [2, 1024, 1024], P(None, None, 'tensor'), may hold values from -0.1875 to 0.1875
- depthwise_weight: bfloat16 [31, 1024], P(None, 'tensor')
- depth_norm_gain: bfloat16 [1024], P('tensor'), may hold values from 0.5 to 1.5
- depth_norm_shift: bfloat16 [1024], P('tensor'), may hold values from -1.5 to 1.5
- pointwise_out: bfloat16 [1024, 1024], P('tensor'), may hold values from -0.25 to 0.25
- second_norm_gain: bfloat16 [1024], replicated, may hold values from 0.5 to 1.5
- second_norm_shift: bfloat16 [1024], replicated, may hold values from -1.5 to 1.5
- second_up_weight: bfloat16 [1024, 4096], P(None, 'tensor'), may hold values from -0.1875 to 0.1875
- second_up_bias: bfloat16 [4096], P('tensor'), may hold values from -1.5 to 1.5
- second_down_weight: bfloat16 [4096, 1024], P('tensor'), may hold values from -0.1875 to 0.1875
- second_down_bias: bfloat16 [1024], replicated, may hold values from -1.5 to 1.5
- final_norm_gain: bfloat16 [1024], replicated, may hold values from 0.5 to 1.5
- final_norm_shift: bfloat16 [1024], replicated, may hold values from -1.5 to 1.5
- cotangent: bfloat16 [32, 512, 1024], P('dp', 'tensor'), may hold values from -6 to 6
Outputs:
- output: bfloat16 [32, 512, 1024], P('dp', 'tensor')
- input_grad: float32 [32, 512, 1024], P('dp', 'tensor')
- grad_first_norm_gain: float32 [1024], replicated
- grad_first_norm_shift: float32 [1024], replicated
- grad_first_up_weight: float32 [1024, 4096], P(None, 'tensor')
- grad_first_up_bias: float32 [4096], P('tensor')
- grad_first_down_weight: float32 [4096, 1024], P('tensor')
- grad_first_down_bias: float32 [1024], replicated
- grad_attend_norm_gain: float32 [1024], replicated
- grad_attend_norm_shift: float32 [1024], replicated
- grad_query_weight: float32 [1024, 1024], P(None, 'tensor')
- grad_query_bias: float32 [1024], P('tensor')
- grad_key_weight: float32 [1024, 1024], P(None, 'tensor')
- grad_value_weight: float32 [1024, 1024], P(None, 'tensor')
- grad_value_bias: float32 [1024], P('tensor')
- grad_output_weight: float32 [1024, 1024], P('tensor')
- grad_output_bias: float32 [1024], replicated
- grad_relative_table: float32 [73, 64], replicated
- grad_convolve_norm_gain: float32 [1024], replicated
- grad_convolve_norm_shift: float32 [1024], replicated
- grad_pointwise_in: float32 [2, 1024, 1024], P(None, None, 'tensor')
- grad_depthwise_weight: float32 [31, 1024], P(None, 'tensor')
- grad_depth_norm_gain: float32 [1024], P('tensor')
- grad_depth_norm_shift: float32 [1024], P('tensor')
- grad_pointwise_out: float32 [1024, 1024], P('tensor')
- grad_second_norm_gain: float32 [1024], replicated
- grad_second_norm_shift: float32 [1024], replicated
- grad_second_up_weight: float32 [1024, 4096], P(None, 'tensor')
- grad_second_up_bias: float32 [4096], P('tensor')
- grad_second_down_weight: float32 [4096, 1024], P('tensor')
- grad_second_down_bias: float32 [1024], replicated
- grad_final_norm_gain: float32 [1024], replicated
- grad_final_norm_shift: float32 [1024], replicated
The draws below stay inside these ranges and needn't reach their ends.
Inputs may be any that keep to these rules, and one draw needn't show every extreme that they name: `clip_count`: for each index of dp, the number of its 2 slots that hold live clips: slots 0 to count - 1 of that index are live and its other slots are ignored; some index holds 2.
All inputs are finite; a program needn't handle non-finite values.
Results may differ from the reference program's by a relative error of at most 0.03.
Values may be sent and summed in bfloat16 or wider, within the bound.
No kernel may reach another device: no remote copies, remote signals or barrier semaphores. Data moves between devices by JAX's collectives and lax.ppermute only.
A program may use at most 384 MiB of HBM per device.

```python
import math
import jax
import jax.numpy as jnp
from jax import lax

D = 1024
HEADS = 16
HEAD_DIM = 64
FF = 4096
CONV_K = 31
BACK = 64
AHEAD = 8
NB = 73
CLIP_LEN = 512
MB = 2
SLOTS = 32
N_DP = 16


def draw_tokens(key, part):
    column_key, row_key, base_key = jax.random.split(jax.random.fold_in(key, 11), 3)
    columns = jnp.exp(jax.random.uniform(column_key, (D,), jnp.float32, -0.5, 0.5) * math.log(10.0))
    rows = jnp.exp(jax.random.uniform(row_key, (SLOTS, CLIP_LEN, 1), jnp.float32, -0.5, 0.5) * math.log(10.0))
    base = jnp.clip(jax.random.normal(base_key, (SLOTS, CLIP_LEN, D), jnp.float32), -4.0, 4.0)
    return (base * rows * columns).astype(jnp.bfloat16)


def draw_depthwise_weight(key, part):
    scale_key, base_key = jax.random.split(jax.random.fold_in(key, 23))
    channels = jnp.exp(jax.random.uniform(scale_key, (D,), jnp.float32, -0.5, 0.5) * math.log(10.0))
    base = jnp.clip(jax.random.normal(base_key, (CONV_K, D), jnp.float32), -4.0, 4.0)
    return (base * channels / math.sqrt(CONV_K)).astype(jnp.bfloat16)


def draw_clip_count(key, part):
    pick_key, rank_key = jax.random.split(jax.random.fold_in(key, 37))
    extra = jax.random.randint(pick_key, (N_DP,), 0, 8)
    counts = jnp.where(extra == 0, MB, 1).astype(jnp.int32)
    forced = jax.random.randint(rank_key, (), 0, N_DP)
    return jnp.where(jnp.arange(N_DP) == forced, MB, counts).astype(jnp.int32)


def steps_of(own_key, dims, cuts, least, top_value):
    factor_of = 1.0
    for dim, parts in cuts:
        draws = jax.random.uniform(jax.random.fold_in(jax.random.fold_in(own_key, 6), dim), (parts,), jnp.float32, least / len(cuts), top_value / len(cuts))
        factor_of = factor_of * jnp.repeat(jnp.exp(draws), dims[dim] // parts).reshape((-1,) + (1,) * (len(dims) - 1 - dim))
    return factor_of


def centred(stream_key, extent, deviation, limit, cuts=(), held_as=jnp.bfloat16):
    array = deviation * jax.random.normal(stream_key, extent, jnp.float32)
    if cuts:
        array = array * steps_of(stream_key, extent, cuts, -0.22, 0.18)
    return jnp.clip(array, -limit, limit).astype(held_as)


def setup_inputs(seed: int = 0) -> dict:
    key_list = jax.random.split(jax.random.key(seed), 35)
    tokens = draw_tokens(jax.random.fold_in(key_list[34], 71), 0)
    clip_count = draw_clip_count(jax.random.fold_in(key_list[34], 71), 0)
    first_norm_gain = jnp.clip(1.0 + 0.1 * jax.random.normal(key_list[2], (D,), jnp.float32), 0.5, 1.5).astype(jnp.bfloat16)
    first_norm_shift = centred(key_list[3], (D,), 0.3, 1.5)
    first_up_weight = centred(key_list[4], (D, FF), D ** -0.5, 0.1875, ((1, 2),))
    first_up_bias = centred(key_list[5], (FF,), 0.3, 1.5, ((0, 2),))
    first_down_weight = centred(key_list[6], (FF, D), (FF // 4) ** -0.5, 0.1875, ((0, 2),))
    first_down_bias = centred(key_list[7], (D,), 0.3, 1.5)
    attend_norm_gain = jnp.clip(1.0 + 0.1 * jax.random.normal(key_list[8], (D,), jnp.float32), 0.5, 1.5).astype(jnp.bfloat16)
    attend_norm_shift = centred(key_list[9], (D,), 0.3, 1.5)
    query_weight = centred(key_list[10], (D, D), D ** -0.5, 0.1875, ((1, 2),))
    query_bias = centred(key_list[11], (D,), 0.3, 1.5, ((0, 2),))
    key_weight = centred(key_list[12], (D, D), D ** -0.5, 0.1875, ((1, 2),))
    value_weight = centred(key_list[13], (D, D), D ** -0.5, 0.1875, ((1, 2),))
    value_bias = centred(key_list[14], (D,), 0.3, 1.5, ((0, 2),))
    output_weight = centred(key_list[15], (D, D), (D // 64) ** -0.5, 1.5, ((0, 2),))
    output_bias = centred(key_list[16], (D,), 0.3, 1.5)
    relative_table = centred(key_list[17], (NB, HEAD_DIM), 1.0, 5.0)
    convolve_norm_gain = jnp.clip(1.0 + 0.1 * jax.random.normal(key_list[18], (D,), jnp.float32), 0.5, 1.5).astype(jnp.bfloat16)
    convolve_norm_shift = centred(key_list[19], (D,), 0.3, 1.5)
    pointwise_in = centred(key_list[20], (2, D, D), D ** -0.5, 0.1875, ((2, 2),))
    depthwise_weight = draw_depthwise_weight(jax.random.fold_in(key_list[34], 71), 0)
    depth_norm_gain = jnp.clip(1.0 + 0.1 * jax.random.normal(key_list[22], (D,), jnp.float32), 0.5, 1.5).astype(jnp.bfloat16)
    depth_norm_shift = centred(key_list[23], (D,), 0.3, 1.5, ((0, 2),))
    pointwise_out = centred(key_list[24], (D, D), (D // 2) ** -0.5, 0.25, ((0, 2),))
    second_norm_gain = jnp.clip(1.0 + 0.1 * jax.random.normal(key_list[25], (D,), jnp.float32), 0.5, 1.5).astype(jnp.bfloat16)
    second_norm_shift = centred(key_list[26], (D,), 0.3, 1.5)
    second_up_weight = centred(key_list[27], (D, FF), D ** -0.5, 0.1875, ((1, 2),))
    second_up_bias = centred(key_list[28], (FF,), 0.3, 1.5, ((0, 2),))
    second_down_weight = centred(key_list[29], (FF, D), (FF // 4) ** -0.5, 0.1875, ((0, 2),))
    second_down_bias = centred(key_list[30], (D,), 0.3, 1.5)
    final_norm_gain = jnp.clip(1.0 + 0.1 * jax.random.normal(key_list[31], (D,), jnp.float32), 0.5, 1.5).astype(jnp.bfloat16)
    final_norm_shift = centred(key_list[32], (D,), 0.3, 1.5)
    cotangent = centred(key_list[33], (SLOTS, CLIP_LEN, D), 1.0, 6.0, ((0, 16), (1, 2)))
    return {"tokens": tokens, "clip_count": clip_count, "first_norm_gain": first_norm_gain, "first_norm_shift": first_norm_shift, "first_up_weight": first_up_weight, "first_up_bias": first_up_bias, "first_down_weight": first_down_weight, "first_down_bias": first_down_bias, "attend_norm_gain": attend_norm_gain, "attend_norm_shift": attend_norm_shift, "query_weight": query_weight, "query_bias": query_bias, "key_weight": key_weight, "value_weight": value_weight, "value_bias": value_bias, "output_weight": output_weight, "output_bias": output_bias, "relative_table": relative_table, "convolve_norm_gain": convolve_norm_gain, "convolve_norm_shift": convolve_norm_shift, "pointwise_in": pointwise_in, "depthwise_weight": depthwise_weight, "depth_norm_gain": depth_norm_gain, "depth_norm_shift": depth_norm_shift, "pointwise_out": pointwise_out, "second_norm_gain": second_norm_gain, "second_norm_shift": second_norm_shift, "second_up_weight": second_up_weight, "second_up_bias": second_up_bias, "second_down_weight": second_down_weight, "second_down_bias": second_down_bias, "final_norm_gain": final_norm_gain, "final_norm_shift": final_norm_shift, "cotangent": cotangent}


@jax.custom_vjp
def low(v):
    return lax.optimization_barrier(v.astype(jnp.bfloat16)).astype(jnp.float32)

@jax.custom_vjp
def low_back(v):
    return v

def low_keep(v):
    return (low(v), None)

def low_pass(kept, grad):
    return (grad,)

def back_keep(v):
    return (v, None)

def back_low(kept, grad):
    return (low(grad),)
low.defvjp(low_keep, low_pass)
low_back.defvjp(back_keep, back_low)
epsilon = 1e-05

def product(left, right):
    return jnp.dot(left, right, precision=lax.Precision.HIGHEST, preferred_element_type=jnp.float32)

def layer_norm(values, gain, shift):
    center = lax.optimization_barrier(jnp.mean(values, axis=-1, keepdims=True))
    offset = values - center
    variance = lax.optimization_barrier(jnp.mean(offset * offset, axis=-1, keepdims=True))
    return offset * lax.rsqrt(variance + epsilon) * gain + shift

def feed_forward(residual, gain, shift, up_weight, up_bias, down_weight, down_bias):
    normed = low(layer_norm(residual, gain, shift))
    before = low_back(product(normed, up_weight)) + up_bias
    hidden = low(before * jax.nn.sigmoid(before))
    branch = low_back(product(hidden, down_weight)) + down_bias
    return residual + 0.5 * branch

def attend(residual, gain, shift, query_weight, query_bias, key_weight, value_weight, value_bias, output_weight, output_bias, relative_table):
    length = residual.shape[0]
    normed = low(layer_norm(residual, gain, shift))
    query = low(low_back(product(normed, query_weight)) + query_bias).reshape(length, HEADS, HEAD_DIM)
    keys = low(low_back(product(normed, key_weight))).reshape(length, HEADS, HEAD_DIM)
    values = low(low_back(product(normed, value_weight)) + value_bias).reshape(length, HEADS, HEAD_DIM)
    content = jnp.einsum('qhe,khe->hqk', query, keys, precision=lax.Precision.HIGHEST)
    relative = jnp.einsum('qhe,re->hqr', query, relative_table, precision=lax.Precision.HIGHEST)
    positions = jnp.arange(length).astype(jnp.int32)
    distance = positions[None, :] - positions[:, None]
    bucket = (jnp.clip(distance, -BACK, AHEAD) + BACK).astype(jnp.int32)
    shifted = jnp.take_along_axis(relative, jnp.broadcast_to(bucket[None], content.shape), axis=2)
    scale = 1.0 / math.sqrt(HEAD_DIM)
    scores = low_back((content + shifted) * scale)
    weights = low(jax.nn.softmax(scores, axis=-1))
    context = jnp.einsum('hqk,khe->qhe', weights, values, precision=lax.Precision.HIGHEST)
    context = low(low_back(context)).reshape(length, D)
    branch = low_back(product(context, output_weight)) + output_bias
    return residual + branch

def convolve(residual, gain, shift, pointwise_in, depthwise, depth_gain, depth_shift, pointwise_out):
    length = residual.shape[0]
    normed = low(layer_norm(residual, gain, shift))
    linear = low_back(product(normed, pointwise_in[0]))
    gating = low_back(product(normed, pointwise_in[1]))
    glu_out = linear * jax.nn.sigmoid(gating)
    padded = jnp.pad(glu_out, ((CONV_K - 1, 0), (0, 0)))
    mixed = jnp.zeros(glu_out.shape, jnp.float32)
    for tap in range(CONV_K):
        mixed = mixed + padded[tap:tap + length] * depthwise[tap]
    shaped = layer_norm(mixed, depth_gain, depth_shift)
    active = low(shaped * jax.nn.sigmoid(shaped))
    return residual + low_back(product(active, pointwise_out))

def sublayers(clip, weights):
    first_gain, first_shift, first_up, first_up_bias, first_down, first_down_bias, attend_gain, attend_shift, query_weight, query_bias, key_weight, value_weight, value_bias, output_weight, output_bias, relative_table, convolve_gain, convolve_shift, pointwise_in, depthwise, depth_gain, depth_shift, pointwise_out, second_gain, second_shift, second_up, second_up_bias, second_down, second_down_bias, final_gain, final_shift = weights
    after_first = feed_forward(clip, first_gain, first_shift, first_up, first_up_bias, first_down, first_down_bias)
    after_attend = attend(after_first, attend_gain, attend_shift, query_weight, query_bias, key_weight, value_weight, value_bias, output_weight, output_bias, relative_table)
    after_convolve = convolve(after_attend, convolve_gain, convolve_shift, pointwise_in, depthwise, depth_gain, depth_shift, pointwise_out)
    after_second = feed_forward(after_convolve, second_gain, second_shift, second_up, second_up_bias, second_down, second_down_bias)
    return layer_norm(after_second, final_gain, final_shift)

def reference(tokens, clip_count, first_norm_gain, first_norm_shift, first_up_weight, first_up_bias, first_down_weight, first_down_bias, attend_norm_gain, attend_norm_shift, query_weight, query_bias, key_weight, value_weight, value_bias, output_weight, output_bias, relative_table, convolve_norm_gain, convolve_norm_shift, pointwise_in, depthwise_weight, depth_norm_gain, depth_norm_shift, pointwise_out, second_norm_gain, second_norm_shift, second_up_weight, second_up_bias, second_down_weight, second_down_bias, final_norm_gain, final_norm_shift, cotangent):
    weights = tuple((value.astype(jnp.float32) for value in (first_norm_gain, first_norm_shift, first_up_weight, first_up_bias, first_down_weight, first_down_bias, attend_norm_gain, attend_norm_shift, query_weight, query_bias, key_weight, value_weight, value_bias, output_weight, output_bias, relative_table, convolve_norm_gain, convolve_norm_shift, pointwise_in, depthwise_weight, depth_norm_gain, depth_norm_shift, pointwise_out, second_norm_gain, second_norm_shift, second_up_weight, second_up_bias, second_down_weight, second_down_bias, final_norm_gain, final_norm_shift)))
    slot_index = jnp.arange(SLOTS).astype(jnp.int32)
    ranks = (slot_index // MB).astype(jnp.int32)
    places = (slot_index % MB).astype(jnp.int32)
    alive = (places < clip_count[ranks]).astype(jnp.float32)

    def one_clip(totals, inputs):
        clip, grad_out, live = inputs
        result, pullback = jax.vjp(sublayers, clip.astype(jnp.float32), weights)
        clip_grad, weight_grads = pullback(grad_out.astype(jnp.float32) * live)
        totals = tuple((left + right for left, right in zip(totals, weight_grads)))
        return (totals, ((result * live).astype(jnp.bfloat16), clip_grad))
    zeros = tuple((jnp.zeros(value.shape, jnp.float32) for value in weights))
    totals, (outputs, input_grads) = lax.scan(one_clip, zeros, (tokens, cotangent, alive))
    clips = jnp.sum(clip_count).astype(jnp.float32)
    return (outputs, input_grads, totals[0] / clips, totals[1] / clips, totals[2] / clips, totals[3] / clips, totals[4] / clips, totals[5] / clips, totals[6] / clips, totals[7] / clips, totals[8] / clips, totals[9] / clips, totals[10] / clips, totals[11] / clips, totals[12] / clips, totals[13] / clips, totals[14] / clips, totals[15] / clips, totals[16] / clips, totals[17] / clips, totals[18] / clips, totals[19] / clips, totals[20] / clips, totals[21] / clips, totals[22] / clips, totals[23] / clips, totals[24] / clips, totals[25] / clips, totals[26] / clips, totals[27] / clips, totals[28] / clips, totals[29] / clips, totals[30] / clips)
```

```python
import math

import jax
import jax.numpy as jnp
from jax import lax
from jax.experimental import pallas as pl
from jax.experimental.pallas import tpu as pltpu
from jax.sharding import PartitionSpec as P

D = 1024
HEAD_DIM = 64
CONV_K = 31
BACK = 64
AHEAD = 8
VMEM_LIMIT = 32 << 20

epsilon = 1e-05


def product(left, right):
    return jnp.dot(left, right, preferred_element_type=jnp.float32)


def product_left(left, right):
    return lax.dot_general(
        left, right, (((0,), (0,)), ((), ())), preferred_element_type=jnp.float32
    )


def product_right(left, right):
    return lax.dot_general(
        left, right, (((1,), (1,)), ((), ())), preferred_element_type=jnp.float32
    )


def widen(value):
    return value.astype(jnp.float32)


def narrow(value):
    return value.astype(jnp.bfloat16)


def norm_stats(values):
    center = jnp.mean(values, axis=-1, keepdims=True)
    offset = values - center
    inverse = lax.rsqrt(jnp.mean(offset * offset, axis=-1, keepdims=True) + epsilon)
    return center, inverse


def layer_norm(values, gain, shift):
    center, inverse = norm_stats(values)
    normal = (values - center) * inverse
    return normal * gain + shift, center, inverse


def norm_back(incoming, normal, inverse, gain):
    scaled = incoming * gain
    first_mean = jnp.mean(scaled, axis=-1, keepdims=True)
    second_mean = jnp.mean(scaled * normal, axis=-1, keepdims=True)
    result = inverse * (scaled - first_mean - normal * second_mean)
    return (result, jnp.sum(incoming * normal, axis=0), jnp.sum(incoming, axis=0))


def paired():
    return lax.axis_size("tensor") == 2


def swap(values):
    return lax.ppermute(values, "tensor", [(0, 1), (1, 0)])


def rows_of(values, which):
    count = values.shape[0] // lax.axis_size("tensor")
    return lax.dynamic_slice_in_dim(values, which * count, count, 0)


def own_rows(values):
    return rows_of(values, lax.axis_index("tensor"))


def wide_sum(share):
    if paired():
        return share + swap(share)
    return lax.psum(share, "tensor")


class Gathered:
    def __init__(self, values):
        self.sent = values

    def move(self, sent):
        if paired():
            return swap(sent)
        return lax.all_gather(sent, "tensor", axis=0, tiled=True)

    def finish(self, sent, got):
        if not paired():
            return got
        first = lax.axis_index("tensor") == 0
        return jnp.concatenate(
            [jnp.where(first, sent, got), jnp.where(first, got, sent)], axis=0
        )


class Summed:
    def __init__(self, share):
        self.sent = narrow(share)

    def move(self, sent):
        if paired():
            return swap(sent)
        return lax.psum(sent, "tensor")

    def finish(self, sent, got):
        if not paired():
            return widen(got)
        return widen(sent) + widen(got)


class Scattered:
    def __init__(self, share):
        self.own = None
        if paired():
            self.own = own_rows(share)
            self.sent = narrow(rows_of(share, 1 - lax.axis_index("tensor")))
        else:
            self.sent = narrow(share)

    def move(self, sent):
        if paired():
            return swap(sent)
        return lax.psum_scatter(sent, "tensor", scatter_dimension=0, tiled=True)

    def finish(self, sent, got):
        if self.own is None:
            return widen(got)
        return self.own + widen(got)


class Job:
    def __init__(self, steps):
        self.steps = steps
        self.result = None
        self.waiting = []
        self.active = True
        self.advance(None)

    def advance(self, values):
        try:
            self.waiting = list(self.steps.send(values))
        except StopIteration as ended:
            self.active = False
            self.waiting = []
            self.result = ended.value


class Flow:
    def __init__(self):
        self.jobs = []

    def launch(self, steps):
        job = Job(steps)
        self.jobs.append(job)
        return job

    def turn(self, held):
        active = [job for job in self.jobs if job.active]
        flat = list(held)
        for job in active:
            flat.extend(job.waiting)
        if len(flat) > 1:
            flat = list(lax.optimization_barrier(tuple(flat)))
        begin = len(held)
        moved = []
        for job in active:
            moved.append(flat[begin : begin + len(job.waiting)])
            begin += len(job.waiting)
        return flat[: len(held)], list(zip(active, moved))

    def run(self, clips):
        under_way = None
        got = {}

        def settle(held):
            extra = [] if under_way is None else [under_way[1].sent, under_way[2]]
            out, moved = self.turn(held + extra)
            if under_way is not None:
                got[under_way[0]] = under_way[1].finish(out[-2], out[-1])
            for job, values in moved:
                job.advance(values)
            return out[: len(held)]

        queue = list(range(len(clips)))
        started = set()
        while queue:
            place = queue.pop(0)
            if under_way is not None and under_way[0] == place:
                settle([])
                under_way = None
            try:
                if place in started:
                    request = clips[place].send(got.pop(place))
                else:
                    started.add(place)
                    request = next(clips[place])
            except StopIteration:
                continue
            (sent,) = settle([request.sent])
            request.sent = sent
            under_way = (place, request, request.move(sent))
            queue.append(place)

    def drain(self):
        while any(job.active for job in self.jobs):
            _, moved = self.turn([])
            for job, values in moved:
                job.advance(values)


def dp_grid():
    return lax.axis_size("dp") == 16


def dp_bit(bit):
    return (lax.axis_index("dp") // bit) % 2


def dp_swap(values, bit):
    return lax.ppermute(values, "dp", [(place, place ^ bit) for place in range(16)])


def piece_of(values, which, axis):
    return lax.dynamic_index_in_dim(values, which, axis, keepdims=False)


def add_low(left, right):
    return narrow(widen(left) + widen(right))


def unstack_columns(shards, values):
    width = shards.shape[-1]
    results = []
    begin = 0
    for value in values:
        size = value.shape[0] // shards.shape[0]
        pieces = []
        for _ in range(0, value.shape[1], width):
            pieces.append(shards[:, begin : begin + size].reshape(value.shape[0], width))
            begin += size
        results.append(jnp.concatenate(pieces, axis=1) if len(pieces) > 1 else pieces[0])
    return results


def split_rows(value):
    return value.reshape(2, 2, 2, 2, value.shape[0] // 16, value.shape[1])


def scatter_job(make, delay, width):
    yield []
    values = yield [narrow(value) for value in make()]
    if not dp_grid():
        return values, [lax.psum(value, "dp") for value in values]
    for _ in range(delay):
        yield []
    parts = []
    for value in values:
        for start in range(0, value.shape[1], width):
            parts.append(split_rows(value[:, start : start + width]))
    core, side, near, far = [dp_bit(bit) for bit in (1, 2, 4, 8)]
    sent = jnp.concatenate([piece_of(part, 1 - core, 3) for part in parts], axis=3)
    kept = jnp.concatenate([piece_of(part, core, 3) for part in parts], axis=3)
    part = add_low(kept, dp_swap(sent, 1))
    (got,) = yield [dp_swap(piece_of(part, 1 - side, 2), 2)]
    part = add_low(piece_of(part, side, 2), got)
    got = dp_swap(piece_of(part, 1 - near, 1), 4)
    part = add_low(piece_of(part, near, 1), got)
    (got,) = yield [dp_swap(piece_of(part, 1 - far, 0), 8)]
    return values, add_low(piece_of(part, far, 0), got)


def gather_job(jobs):
    while any(job.active for job in jobs):
        yield []
    if not dp_grid():
        return [value for job in jobs for value in job.result[1]]
    shards = jnp.concatenate([job.result[1] for job in jobs], axis=0)
    whole = lax.all_gather(shards, "dp", axis=0)
    return unstack_columns(whole, [value for job in jobs for value in job.result[0]])


def small_job(values):
    flat = jnp.concatenate([value.reshape(-1) for value in values])
    if dp_grid():
        for bit in (1, 2, 4, 8):
            (got,) = yield [dp_swap(flat, bit)]
            flat = flat + got
    else:
        flat = lax.psum(flat, "dp")
    results = []
    start = 0
    for value in values:
        results.append(flat[start : start + value.size].reshape(value.shape))
        start += value.size
    return results


SCALE = 1.0 / math.sqrt(HEAD_DIM)
PAIR = 2 * HEAD_DIM
QB = 128
WINDOW = 3 * QB


def keep_head(block, head):
    inside = lax.broadcasted_iota(jnp.int32, block.shape, 1) < HEAD_DIM
    if head == 1:
        inside = jnp.logical_not(inside)
    return jnp.where(inside, block, jnp.zeros_like(block))


def window_place():
    return lax.broadcasted_iota(jnp.int32, (QB, WINDOW), 1) - lax.broadcasted_iota(
        jnp.int32, (QB, WINDOW), 0
    )


def spread_rows(relative, block, blocks):
    low = max(block - 1, 0)
    high = min(block + 2, blocks)
    before = relative[:, 0:1]
    after = relative[:, BACK + AHEAD : BACK + AHEAD + 1]
    wide = jnp.concatenate([relative, jnp.zeros((QB, WINDOW - QB), jnp.float32)], axis=1)
    skewed = pltpu.roll(wide, QB - BACK, 1, stride=1, stride_axis=0)
    place = window_place()
    skewed = jnp.where(place < QB - BACK, before, skewed)
    skewed = jnp.where(place > QB + AHEAD, after, skewed)
    parts = []
    if low > 0:
        parts.append(jnp.broadcast_to(before, (QB, low * QB)))
    parts.append(skewed[:, (low - block + 1) * QB : (high - block + 1) * QB])
    if high < blocks:
        parts.append(jnp.broadcast_to(after, (QB, (blocks - high) * QB)))
    return jnp.concatenate(parts, axis=1)


def gather_rows_back(incoming, block, blocks, flip):
    low = max(block - 1, 0)
    high = min(block + 2, blocks)
    wide = widen(incoming)
    place = lax.broadcasted_iota(jnp.int32, wide.shape, 1) - lax.broadcasted_iota(
        jnp.int32, wide.shape, 0
    )
    back = jnp.sum(
        jnp.where(place <= block * QB - BACK, wide, 0.0), axis=-1, keepdims=True
    )
    ahead = jnp.sum(
        jnp.where(place >= block * QB + AHEAD, wide, 0.0), axis=-1, keepdims=True
    )
    parts = []
    if block == 0:
        parts.append(jnp.zeros((QB, QB), jnp.bfloat16))
    parts.append(incoming[:, low * QB : high * QB])
    if block == blocks - 1:
        parts.append(jnp.zeros((QB, QB), jnp.bfloat16))
    window = jnp.concatenate(parts, axis=1)
    reversed_rows = product(flip, window)
    moved = pltpu.roll(
        reversed_rows, WINDOW - (QB - BACK) - (QB - 1), 1, stride=1, stride_axis=0
    )[:, :QB]
    inner = product(flip, narrow(moved))
    lane = lax.broadcasted_iota(jnp.int32, (QB, QB), 1)
    inner = jnp.where(lane < BACK + AHEAD, inner, 0.0)
    inner = jnp.where(lane == 0, back, inner)
    return jnp.where(lane == BACK + AHEAD, ahead, inner)


def block_rows(block):
    return slice(block * QB, (block + 1) * QB)


def softmax_rows(content, relative, block, blocks):
    scores = (content + spread_rows(relative, block, blocks)) * SCALE
    weights = jnp.exp(scores - jnp.max(scores, axis=-1, keepdims=True))
    return weights * (1.0 / jnp.sum(weights, axis=-1, keepdims=True))


def scores_of(query_head, key_block, table_block, blocks):
    content = product_right(query_head, key_block)
    relative = product(query_head, table_block)
    rows = [
        spread_rows(relative[block * QB : (block + 1) * QB], block, blocks)
        for block in range(blocks)
    ]
    return (content + jnp.concatenate(rows, axis=0)) * SCALE


def softmax_of(scores):
    weights = jnp.exp(scores - jnp.max(scores, axis=-1, keepdims=True))
    return weights * (1.0 / jnp.sum(weights, axis=-1, keepdims=True))


def attend_kernel(query_ref, key_ref, value_ref, table_ref, context_ref):
    blocks = query_ref.shape[0] // QB
    query = query_ref[...]
    keys = key_ref[...]
    values = value_ref[...]
    table = table_ref[...]
    parts = []
    for head in range(2):
        probs = softmax_of(scores_of(keep_head(query, head), keys, table, blocks))
        parts.append(product(probs.astype(jnp.bfloat16), values))
    lane = lax.broadcasted_iota(jnp.int32, parts[0].shape, 1)
    context_ref[...] = jnp.where(lane < HEAD_DIM, parts[0], parts[1]).astype(jnp.bfloat16)


def attend_back_kernel(
    query_ref,
    key_ref,
    value_ref,
    grad_ref,
    table_ref,
    rows_ref,
    query_grad_ref,
    key_grad_ref,
    value_grad_ref,
    query_sum_ref,
    value_sum_ref,
    table_grad_ref,
    score_ref,
    wide_ref,
    probs_ref,
    low_ref,
    band_ref,
):
    @pl.when(pl.program_id(0) == 0)
    def _():
        table_grad_ref[...] = jnp.zeros_like(table_grad_ref)

    blocks = query_ref.shape[0] // QB
    query_turned = narrow(widen(query_ref[...]).T)
    grad_turned = narrow(widen(grad_ref[...]).T)
    flip = narrow(
        (
            lax.broadcasted_iota(jnp.int32, (QB, QB), 0)
            + lax.broadcasted_iota(jnp.int32, (QB, QB), 1)
            == QB - 1
        ).astype(jnp.float32)
    )
    query_parts = []
    key_parts = []
    value_parts = []
    for head in range(2):
        piece = slice(head * HEAD_DIM, (head + 1) * HEAD_DIM)
        query = keep_head(query_ref[...], head)
        score_ref[head] = product_right(query, key_ref[...])
        relative = product(query, table_ref[...])
        wide_ref[head] = product_right(keep_head(grad_ref[...], head), value_ref[...])
        for block in range(blocks):
            rows = block_rows(block)
            probs = softmax_rows(score_ref[head, rows], relative[rows], block, blocks)
            probs_ref[head, rows] = narrow(probs)
            probs_grad = wide_ref[head, rows]
            delta = jnp.sum(probs * probs_grad, axis=-1, keepdims=True)
            score_grad = narrow(probs * (probs_grad - delta))
            low_ref[head, rows] = score_grad
            band_ref[head, rows] = gather_rows_back(score_grad, block, blocks, flip)
        value_parts.append(product(grad_turned[piece], probs_ref[head]))
        key_parts.append(product(query_turned[piece], low_ref[head]))
        band = band_ref[head]
        band_high = narrow(band)
        band_low = narrow(band - widen(band_high))
        query_parts.append(
            product(low_ref[head], key_ref[...])
            + product(band_high, rows_ref[...])
            + product(band_low, rows_ref[...])
        )
        table_grad_ref[...] += SCALE * (
            product(query_turned[piece], band_high) + product(query_turned[piece], band_low)
        )
    lane = lax.broadcasted_iota(jnp.int32, query_parts[0].shape, 1)
    query_grad = SCALE * jnp.where(lane < HEAD_DIM, query_parts[0], query_parts[1])
    query_grad_ref[...] = narrow(query_grad)
    query_sum_ref[...] = jnp.sum(query_grad, axis=0, keepdims=True)
    key_grad_ref[...] = narrow(SCALE * jnp.concatenate(key_parts, axis=0).T)
    value_grad = jnp.concatenate(value_parts, axis=0).T
    value_grad_ref[...] = narrow(value_grad)
    value_sum_ref[...] = jnp.sum(value_grad, axis=0, keepdims=True)


def pair_spec(length):
    return pl.BlockSpec((length, PAIR), lambda pair: (0, pair))


def fixed_spec(shape):
    return pl.BlockSpec(shape, lambda pair: tuple(0 for _ in shape))


def table_forms(relative_table):
    padded = jnp.pad(relative_table, ((0, QB - relative_table.shape[0]), (0, 0)))
    rows = jnp.concatenate([padded, padded], axis=1)
    return rows.T, rows


def attend_heads(query, keys, values, table):
    length, width = query.shape
    return pl.pallas_call(
        attend_kernel,
        out_shape=jax.ShapeDtypeStruct((length, width), jnp.bfloat16),
        grid=(width // PAIR,),
        in_specs=[pair_spec(length)] * 3 + [fixed_spec((PAIR, QB))],
        out_specs=pair_spec(length),
        compiler_params=pltpu.CompilerParams(vmem_limit_bytes=VMEM_LIMIT),
        name="attend_heads",
    )(query, keys, values, table)


def attend_heads_back(query, keys, values, grad, table, rows):
    length, width = query.shape
    sums = pl.BlockSpec((1, PAIR), lambda pair: (0, pair))
    return pl.pallas_call(
        attend_back_kernel,
        out_shape=(
            jax.ShapeDtypeStruct((length, width), jnp.bfloat16),
            jax.ShapeDtypeStruct((length, width), jnp.bfloat16),
            jax.ShapeDtypeStruct((length, width), jnp.bfloat16),
            jax.ShapeDtypeStruct((1, width), jnp.float32),
            jax.ShapeDtypeStruct((1, width), jnp.float32),
            jax.ShapeDtypeStruct((HEAD_DIM, QB), jnp.float32),
        ),
        grid=(width // PAIR,),
        in_specs=[pair_spec(length)] * 4 + [fixed_spec((PAIR, QB)), fixed_spec((QB, PAIR))],
        out_specs=(pair_spec(length),) * 3 + (sums, sums, fixed_spec((HEAD_DIM, QB))),
        scratch_shapes=[
            pltpu.VMEM((2, length, length), jnp.float32),
            pltpu.VMEM((2, length, length), jnp.float32),
            pltpu.VMEM((2, length, length), jnp.bfloat16),
            pltpu.VMEM((2, length, length), jnp.bfloat16),
            pltpu.VMEM((2, length, QB), jnp.float32),
        ],
        compiler_params=pltpu.CompilerParams(vmem_limit_bytes=VMEM_LIMIT),
        name="attend_heads_back",
    )(query, keys, values, grad, table, rows)
LANES = 128
STRIP = 64
EDGE = 32


def mix_kernel(linear_ref, gate_ref, taps_ref, mixed_ref, sums_ref, padded_ref, total_ref):
    length = linear_ref.shape[0]
    padded_ref[0:EDGE] = jnp.zeros((EDGE, LANES), jnp.float32)
    padded_ref[EDGE : EDGE + length] = linear_ref[...] * jax.nn.sigmoid(gate_ref[...])

    def strip(index, carry):
        begin = pl.multiple_of(index * STRIP, STRIP)
        total = jnp.zeros((STRIP, LANES), jnp.float32)
        for tap in range(CONV_K):
            total = total + padded_ref[
                pl.ds(begin + EDGE - CONV_K + 1 + tap, STRIP), :
            ] * taps_ref[tap : tap + 1, :]
        mixed_ref[pl.ds(begin, STRIP), :] = total
        return carry

    lax.fori_loop(0, length // STRIP, strip, 0)
    mixed = mixed_ref[...]

    @pl.when(pl.program_id(0) == 0)
    def _():
        total_ref[...] = jnp.zeros_like(total_ref)

    total_ref[0] += mixed
    total_ref[1] += mixed * mixed

    @pl.when(pl.program_id(0) == pl.num_programs(0) - 1)
    def _():
        ones = jnp.ones((8, LANES), jnp.float32)
        sums_ref[...] = jnp.concatenate(
            [
                lax.dot_general(
                    ones,
                    total_ref[place],
                    (((1,), (1,)), ((), ())),
                    precision=lax.Precision.HIGHEST,
                    preferred_element_type=jnp.float32,
                )
                for place in range(2)
            ],
            axis=0,
        )


def mix_channels(linear, gate, taps):
    length, width = linear.shape
    block = pl.BlockSpec((length, LANES), lambda part: (0, part))
    mixed, sums = pl.pallas_call(
        mix_kernel,
        out_shape=(
            jax.ShapeDtypeStruct((length, width), jnp.float32),
            jax.ShapeDtypeStruct((16, length), jnp.float32),
        ),
        grid=(width // LANES,),
        in_specs=[block, block, pl.BlockSpec((EDGE, LANES), lambda part: (0, part))],
        out_specs=(block, pl.BlockSpec((16, length), lambda part: (0, 0))),
        scratch_shapes=[
            pltpu.VMEM((EDGE + length, LANES), jnp.float32),
            pltpu.VMEM((2, length, LANES), jnp.float32),
        ],
        compiler_params=pltpu.CompilerParams(vmem_limit_bytes=VMEM_LIMIT),
        name="mix_channels",
    )(linear, gate, taps)
    return mixed, jnp.concatenate([sums[0:1], sums[8:9]], axis=0)


def mix_back_kernel(
    grad_ref,
    linear_ref,
    gate_ref,
    taps_ref,
    linear_grad_ref,
    gating_grad_ref,
    taps_grad_ref,
    padded_ref,
    tail_ref,
    total_ref,
):
    length = linear_ref.shape[0]
    padded_ref[0:EDGE] = jnp.zeros((EDGE, LANES), jnp.float32)
    padded_ref[EDGE : EDGE + length] = linear_ref[...] * jax.nn.sigmoid(gate_ref[...])
    tail_ref[0:length] = grad_ref[...]
    tail_ref[length : length + EDGE] = jnp.zeros((EDGE, LANES), jnp.float32)
    total_ref[...] = jnp.zeros_like(total_ref)

    def strip(index, carry):
        begin = pl.multiple_of(index * STRIP, STRIP)
        here = pl.ds(begin, STRIP)
        grad = tail_ref[here, :]
        total = jnp.zeros((STRIP, LANES), jnp.float32)
        for tap in range(CONV_K):
            total = total + tail_ref[
                pl.ds(begin + CONV_K - 1 - tap, STRIP), :
            ] * taps_ref[tap : tap + 1, :]
            weighed = grad * padded_ref[pl.ds(begin + EDGE - CONV_K + 1 + tap, STRIP), :]
            total_ref[tap] += jnp.sum(weighed.reshape(STRIP // 8, 8, LANES), axis=0)
        sigma = jax.nn.sigmoid(gate_ref[here, :])
        low = total * sigma
        linear_grad_ref[here, :] = narrow(low)
        gating_grad_ref[here, :] = narrow(low * linear_ref[here, :] * (1.0 - sigma))
        return carry

    lax.fori_loop(0, length // STRIP, strip, 0)
    for tap in range(CONV_K):
        taps_grad_ref[tap : tap + 1, :] = jnp.sum(total_ref[tap], axis=0, keepdims=True)
    taps_grad_ref[CONV_K:EDGE, :] = jnp.zeros((EDGE - CONV_K, LANES), jnp.float32)


def mix_channels_back(grad, linear, gate, taps):
    length, width = linear.shape
    block = pl.BlockSpec((length, LANES), lambda part: (0, part))
    edge = pl.BlockSpec((EDGE, LANES), lambda part: (0, part))
    return pl.pallas_call(
        mix_back_kernel,
        out_shape=(
            jax.ShapeDtypeStruct((length, width), jnp.bfloat16),
            jax.ShapeDtypeStruct((length, width), jnp.bfloat16),
            jax.ShapeDtypeStruct((EDGE, width), jnp.float32),
        ),
        grid=(width // LANES,),
        in_specs=[block, block, block, edge],
        out_specs=(block, block, edge),
        scratch_shapes=[
            pltpu.VMEM((EDGE + length, LANES), jnp.float32),
            pltpu.VMEM((EDGE + length, LANES), jnp.float32),
            pltpu.VMEM((EDGE, 8, LANES), jnp.float32),
        ],
        compiler_params=pltpu.CompilerParams(vmem_limit_bytes=VMEM_LIMIT),
        name="mix_channels_back",
    )(grad, linear, gate, taps)


def feed_forward(rows, gain, shift, up_weight, up_bias, down_weight):
    normed, center, inverse = layer_norm(rows, gain, shift)
    normed = narrow(normed)
    before = product(normed, up_weight) + up_bias
    hidden = narrow(before * jax.nn.sigmoid(before))
    return product(hidden, down_weight), (rows, center, inverse, normed, before, hidden)


def feed_back(incoming, kept, up_weight, down_weight):
    before = kept[4]
    branch_grad = 0.5 * incoming
    spread = narrow(branch_grad)
    sigma = jax.nn.sigmoid(before)
    before_grad = product_right(spread, down_weight) * sigma * (1.0 + before * (1.0 - sigma))
    before_low = narrow(before_grad)
    share = product_right(before_low, up_weight)
    return share, spread, before_low, jnp.sum(before_grad, axis=0), jnp.sum(branch_grad, axis=0)


def residual_back(incoming, normed_grad, kept, gain):
    rows, center, inverse = kept[:3]
    normal = (rows - center) * inverse
    result, gain_grad, shift_grad = norm_back(normed_grad, normal, inverse, gain)
    return incoming + result, gain_grad, shift_grad


def attend(
    rows, gain, shift, query_weight, query_bias, key_weight, value_weight, value_bias, output_weight, table
):
    normed, center, inverse = layer_norm(rows, gain, shift)
    normed = narrow(normed)
    query = narrow(product(normed, query_weight) + query_bias)
    keys = narrow(product(normed, key_weight))
    values = narrow(product(normed, value_weight) + value_bias)
    context = attend_heads(query, keys, values, table)
    return (
        product(context, output_weight),
        (rows, center, inverse, normed, query, keys, values, context),
    )


def attend_back(
    incoming, kept, query_weight, key_weight, value_weight, output_weight, table, table_rows
):
    query, keys, values = kept[4:7]
    spread = narrow(incoming)
    context_grad = narrow(product_right(spread, output_weight))
    query_low, key_low, value_low, query_sum, value_sum, table_grad = attend_heads_back(
        query, keys, values, context_grad, table, table_rows
    )
    share = (
        product_right(query_low, query_weight)
        + product_right(key_low, key_weight)
        + product_right(value_low, value_weight)
    )
    return (
        share,
        spread,
        (query_low, key_low, value_low),
        query_sum[0],
        value_sum[0],
        jnp.sum(incoming, axis=0),
        table_grad,
    )


def mix(rows, gain, shift, pointwise_in, taps):
    normed, center, inverse = layer_norm(rows, gain, shift)
    normed = narrow(normed)
    linear = product(normed, pointwise_in[0])
    gate = product(normed, pointwise_in[1])
    mixed, sums = mix_channels(linear, gate, taps)
    return mixed, wide_sum(sums), (rows, center, inverse, normed, linear, gate)


def convolve(mixed, sums, depth_gain, depth_shift, pointwise_out):
    center = (sums[0] / D)[:, None]
    channel_inverse = lax.rsqrt(sums[1][:, None] / D - center * center + epsilon)
    channel_normal = (mixed - center) * channel_inverse
    shaped = channel_normal * depth_gain + depth_shift
    active = narrow(shaped * jax.nn.sigmoid(shaped))
    return product(active, pointwise_out), (channel_inverse, channel_normal, shaped, active)


def shape_back(incoming, shape_kept, depth_gain, pointwise_out):
    channel_inverse, channel_normal, shaped, active = shape_kept
    spread = narrow(incoming)
    sigma = jax.nn.sigmoid(shaped)
    shaped_grad = product_right(spread, pointwise_out) * sigma * (1.0 + shaped * (1.0 - sigma))
    scaled = shaped_grad * depth_gain
    sums = wide_sum(
        jnp.stack([jnp.sum(scaled, axis=-1), jnp.sum(scaled * channel_normal, axis=-1)])
    )
    return (
        spread,
        scaled,
        sums,
        jnp.sum(shaped_grad * channel_normal, axis=0),
        jnp.sum(shaped_grad, axis=0),
    )


def convolve_back(scaled, sums, kept, shape_kept, pointwise_in, taps):
    linear, gate = kept[4:6]
    channel_inverse, channel_normal = shape_kept[:2]
    mixed_grad = channel_inverse * (
        scaled - (sums[0] / D)[:, None] - channel_normal * (sums[1] / D)[:, None]
    )
    linear_low, gating_low, taps_grad = mix_channels_back(mixed_grad, linear, gate, taps)
    share = product_right(linear_low, pointwise_in[0]) + product_right(gating_low, pointwise_in[1])
    return share, linear_low, gating_low, taps_grad[:CONV_K]


def total(parts):
    result = parts[0]
    for part in parts[1:]:
        result = result + part
    return result


def weight_grad(lefts, rights):
    return total([product_left(left, right) for left, right in zip(lefts, rights)])


class Gradients:
    def __init__(self, flow, count):
        self.flow = flow
        self.count = count
        self.parts = {}
        self.jobs = {}

    def add(self, name, part):
        parts = self.parts.setdefault(name, [])
        parts.append(part)
        return len(parts) == self.count

    def weights(self, name, pairs, width, delay=0):
        if self.add(name, pairs):
            parts = self.parts[name]

            def make():
                return [
                    weight_grad([part[place][0] for part in parts], [part[place][1] for part in parts])
                    for place in range(len(pairs))
                ]

            self.jobs[name] = self.flow.launch(scatter_job(make, delay, width))

    def sums(self, name, values):
        self.add(name, values)

    def reduce_sums(self, name, groups):
        values = []
        for group in groups:
            parts = self.parts[group]
            values.extend(total([part[place] for part in parts]) for place in range(len(parts[0])))
        self.jobs[name] = self.flow.launch(small_job(values))

    def gather(self, name, members):
        if members[-1] in self.jobs and name not in self.jobs:
            self.jobs[name] = self.flow.launch(
                gather_job([self.jobs[member] for member in members])
            )

    def result(self, name):
        return self.jobs[name].result


def per_device(
    tokens,
    clip_count,
    first_norm_gain,
    first_norm_shift,
    first_up_weight,
    first_up_bias,
    first_down_weight,
    first_down_bias,
    attend_norm_gain,
    attend_norm_shift,
    query_weight,
    query_bias,
    key_weight,
    value_weight,
    value_bias,
    output_weight,
    output_bias,
    relative_table,
    convolve_norm_gain,
    convolve_norm_shift,
    pointwise_in,
    depthwise_weight,
    depth_norm_gain,
    depth_norm_shift,
    pointwise_out,
    second_norm_gain,
    second_norm_shift,
    second_up_weight,
    second_up_bias,
    second_down_weight,
    second_down_bias,
    final_norm_gain,
    final_norm_shift,
    cotangent,
):
    slots = range(tokens.shape[0])
    live_count = clip_count[0]
    first_gain = widen(first_norm_gain)
    attend_gain = widen(attend_norm_gain)
    convolve_gain = widen(convolve_norm_gain)
    second_gain = widen(second_norm_gain)
    final_gain = widen(final_norm_gain)
    taps = jnp.pad(widen(depthwise_weight), ((0, EDGE - CONV_K), (0, 0)))
    depth_gain = widen(depth_norm_gain)
    table, table_rows = table_forms(relative_table)
    flow = Flow()
    grads = Gradients(flow, len(slots))
    outputs = {}
    input_grads = {}
    count_job = flow.launch(small_job([jnp.full((1, 128), widen(live_count), jnp.float32)]))

    def clip(slot):
        live = (live_count > slot).astype(jnp.float32)
        rows = widen((yield Gathered(tokens[slot])))
        share, first_kept = feed_forward(
            rows,
            first_gain,
            widen(first_norm_shift),
            first_up_weight,
            widen(first_up_bias),
            first_down_weight,
        )
        rows = rows + 0.5 * ((yield Summed(share)) + widen(first_down_bias))
        share, attend_kept = attend(
            rows,
            attend_gain,
            widen(attend_norm_shift),
            query_weight,
            widen(query_bias),
            key_weight,
            value_weight,
            widen(value_bias),
            output_weight,
            table,
        )
        rows = rows + (yield Summed(share)) + widen(output_bias)
        mixed, sums, convolve_kept = mix(
            rows, convolve_gain, widen(convolve_norm_shift), pointwise_in, taps
        )
        share, shape_kept = convolve(
            mixed, sums, depth_gain, widen(depth_norm_shift), pointwise_out
        )
        rows = rows + (yield Summed(share))
        share, second_kept = feed_forward(
            rows,
            second_gain,
            widen(second_norm_shift),
            second_up_weight,
            widen(second_up_bias),
            second_down_weight,
        )
        last = own_rows(rows) + 0.5 * ((yield Scattered(share)) + widen(second_down_bias))
        normed, center, inverse = layer_norm(last, final_gain, widen(final_norm_shift))
        outputs[slot] = narrow(normed * live)
        grad, gain_grad, shift_grad = norm_back(
            widen(cotangent[slot]) * live, (last - center) * inverse, inverse, final_gain
        )
        grads.sums("final", [gain_grad, shift_grad])

        grad = widen((yield Gathered(narrow(grad))))
        share, spread, before_low, up_sum, down_sum = feed_back(
            grad, second_kept, second_up_weight, second_down_weight
        )
        grads.weights("second_down", [(second_kept[5], spread)], spread.shape[1])
        grads.weights("second_up", [(second_kept[3], before_low)], spread.shape[1], 1)
        grads.gather("second", ["second_down", "second_up"])
        normed_grad = yield Summed(share)
        grad, gain_grad, shift_grad = residual_back(grad, normed_grad, second_kept, second_gain)
        grads.sums("second", [up_sum, down_sum, gain_grad, shift_grad])

        spread, scaled, sums, depth_gain_sum, depth_shift_sum = shape_back(
            grad, shape_kept, depth_gain, pointwise_out
        )
        share, linear_low, gating_low, depthwise_sum = convolve_back(
            scaled, sums, convolve_kept, shape_kept, pointwise_in, taps
        )
        grads.weights(
            "convolve",
            [
                (convolve_kept[3], linear_low),
                (convolve_kept[3], gating_low),
                (shape_kept[3], spread),
            ],
            linear_low.shape[1],
        )
        normed_grad = yield Summed(share)
        grad, gain_grad, shift_grad = residual_back(
            grad, normed_grad, convolve_kept, convolve_gain
        )
        grads.sums(
            "convolve_sums", [depth_gain_sum, depth_shift_sum, depthwise_sum, gain_grad, shift_grad]
        )

        share, spread, lows, query_sum, value_sum, output_sum, table_sum = attend_back(
            grad,
            attend_kept,
            query_weight,
            key_weight,
            value_weight,
            output_weight,
            table,
            table_rows,
        )
        grads.weights(
            "attend",
            [(attend_kept[7], spread)] + [(attend_kept[3], low) for low in lows],
            lows[0].shape[1],
        )
        grads.sums("attend_sums", [query_sum, value_sum, output_sum, table_sum])
        if slot == slots[-1]:
            grads.parts["final"] = [
                list(wide_sum(total([jnp.stack(part) for part in grads.parts["final"]])))
            ]
            grads.reduce_sums("early", ["final", "second", "convolve_sums", "attend_sums"])
        grads.gather("middle", ["convolve", "attend"])
        normed_grad = yield Summed(share)
        grad, gain_grad, shift_grad = residual_back(grad, normed_grad, attend_kept, attend_gain)
        grads.sums("attend_norm", [gain_grad, shift_grad])

        share, spread, before_low, up_sum, down_sum = feed_back(
            grad, first_kept, first_up_weight, first_down_weight
        )
        grads.weights("first_down", [(first_kept[5], spread)], spread.shape[1])
        grads.weights("first_up", [(first_kept[3], before_low)], spread.shape[1], 1)
        grads.gather("first_both", ["first_down", "first_up"])
        normed_grad = yield Scattered(share)
        input_grads[slot], gain_grad, shift_grad = residual_back(
            own_rows(grad),
            normed_grad,
            [own_rows(kept) for kept in first_kept[:3]],
            first_gain,
        )
        grads.sums("first", [up_sum, down_sum])
        grads.sums("first_norm", [gain_grad, shift_grad])

    flow.run([clip(slot) for slot in slots])
    grads.parts["first_norm"] = [
        list(wide_sum(total([jnp.stack(part) for part in grads.parts["first_norm"]])))
    ]
    grads.reduce_sums("late", ["attend_norm", "first", "first_norm"])
    flow.drain()

    clips = count_job.result[0][0, 0]
    early = grads.result("early")
    late = grads.result("late")
    second_down, second_up = grads.result("second")
    linear, gating, point_out, output_grad, query_grad, key_grad, value_grad = grads.result("middle")
    first_down, first_up = grads.result("first_both")
    table_grad = wide_sum(early[14]).T[: relative_table.shape[0]]
    every = (
        late[4],
        late[5],
        first_up,
        late[2],
        first_down,
        late[3],
        late[0],
        late[1],
        query_grad,
        early[11],
        key_grad,
        value_grad,
        early[12],
        output_grad,
        early[13],
        table_grad,
        early[9],
        early[10],
        jnp.stack([linear, gating]),
        early[8],
        early[6],
        early[7],
        point_out,
        early[4],
        early[5],
        second_up,
        early[2],
        second_down,
        early[3],
        early[0],
        early[1],
    )
    return (
        jnp.stack([outputs[slot] for slot in slots]),
        jnp.stack([input_grads[slot] for slot in slots]),
    ) + tuple(widen(value) / clips for value in every)


def solution(mesh):
    placed = (
        P("dp", "tensor", None),
        P("dp"),
        P(),
        P(),
        P(None, "tensor"),
        P("tensor"),
        P("tensor", None),
        P(),
        P(),
        P(),
        P(None, "tensor"),
        P("tensor"),
        P(None, "tensor"),
        P(None, "tensor"),
        P("tensor"),
        P("tensor", None),
        P(),
        P(),
        P(),
        P(),
        P(None, None, "tensor"),
        P(None, "tensor"),
        P("tensor"),
        P("tensor"),
        P("tensor", None),
        P(),
        P(),
        P(None, "tensor"),
        P("tensor"),
        P("tensor", None),
        P(),
        P(),
        P(),
        P("dp", "tensor", None),
    )
    return jax.shard_map(
        per_device,
        mesh=mesh,
        in_specs=placed,
        out_specs=(
            P("dp", "tensor", None),
            P("dp", "tensor", None),
            P(),
            P(),
            P(None, "tensor"),
            P("tensor"),
            P("tensor", None),
            P(),
            P(),
            P(),
            P(None, "tensor"),
            P("tensor"),
            P(None, "tensor"),
            P(None, "tensor"),
            P("tensor"),
            P("tensor", None),
            P(),
            P(),
            P(),
            P(),
            P(None, None, "tensor"),
            P(None, "tensor"),
            P("tensor"),
            P("tensor"),
            P("tensor", None),
            P(),
            P(),
            P(None, "tensor"),
            P("tensor"),
            P("tensor", None),
            P(),
            P(),
            P(),
        ),
        check_vma=False,
    )
```

```python
import functools
import math

import jax
import jax.numpy as jnp
from jax import lax
from jax.experimental import pallas as pl
from jax.experimental.pallas import tpu as pltpu
from jax.sharding import PartitionSpec as P

D = 1024
HEAD_DIM = 64
CONV_K = 31
BACK = 64
AHEAD = 8

epsilon = 1e-05


def product(left, right):
    return jnp.dot(left, right, preferred_element_type=jnp.float32)


def product_left(left, right):
    return lax.dot_general(
        left, right, (((0,), (0,)), ((), ())), preferred_element_type=jnp.float32
    )


def product_right(left, right):
    return lax.dot_general(
        left, right, (((1,), (1,)), ((), ())), preferred_element_type=jnp.float32
    )


def widen(value):
    return value.astype(jnp.float32)


def narrow(value):
    return value.astype(jnp.bfloat16)


def norm_stats(values):
    center = jnp.mean(values, axis=-1, keepdims=True)
    offset = values - center
    inverse = lax.rsqrt(jnp.mean(offset * offset, axis=-1, keepdims=True) + epsilon)
    return center, inverse


def layer_norm(values, gain, shift):
    center, inverse = norm_stats(values)
    normal = (values - center) * inverse
    return normal * gain + shift, center, inverse


def norm_back(incoming, normal, inverse, gain):
    scaled = incoming * gain
    first_mean = jnp.mean(scaled, axis=-1, keepdims=True)
    second_mean = jnp.mean(scaled * normal, axis=-1, keepdims=True)
    result = inverse * (scaled - first_mean - normal * second_mean)
    return (result, jnp.sum(incoming * normal, axis=0), jnp.sum(incoming, axis=0))


def paired():
    return lax.axis_size("tensor") == 2


def swap(values):
    return lax.ppermute(values, "tensor", [(0, 1), (1, 0)])


def rows_of(values, which):
    count = values.shape[0] // lax.axis_size("tensor")
    return lax.dynamic_slice_in_dim(values, which * count, count, 0)


def own_rows(values):
    return rows_of(values, lax.axis_index("tensor"))


def wide_sum(share):
    if paired():
        count = 2 * lax.axis_size("dp")
        pairs = [(place, place ^ 1) for place in reversed(range(count))]
        return share + lax.ppermute(share, ("dp", "tensor"), pairs)
    return lax.psum(share, "tensor")


class Gathered:
    def __init__(self, values):
        self.sent = values

    def move(self, sent):
        if paired():
            return swap(sent)
        return lax.all_gather(sent, "tensor", axis=0, tiled=True)

    def finish(self, sent, got):
        if not paired():
            return got
        first = lax.axis_index("tensor") == 0
        return jnp.concatenate(
            [jnp.where(first, sent, got), jnp.where(first, got, sent)], axis=0
        )


class Summed:
    def __init__(self, share):
        self.sent = narrow(share)

    def move(self, sent):
        if paired():
            return swap(sent)
        return lax.psum(sent, "tensor")

    def finish(self, sent, got):
        if not paired():
            return widen(got)
        return widen(sent) + widen(got)


class Scattered:
    def __init__(self, share):
        self.own = None
        if paired():
            self.own = own_rows(share)
            self.sent = narrow(rows_of(share, 1 - lax.axis_index("tensor")))
        else:
            self.sent = narrow(share)

    def move(self, sent):
        if paired():
            return swap(sent)
        return lax.psum_scatter(sent, "tensor", scatter_dimension=0, tiled=True)

    def finish(self, sent, got):
        if self.own is None:
            return widen(got)
        return self.own + widen(got)


class Met:
    def __init__(self, values):
        self.values = list(values)


class Job:
    def __init__(self, steps):
        self.steps = steps
        self.result = None
        self.waiting = []
        self.active = True
        self.advance(None)

    def advance(self, values):
        try:
            self.waiting = list(self.steps.send(values))
        except StopIteration as ended:
            self.active = False
            self.waiting = []
            self.result = ended.value


class Flow:
    def __init__(self):
        self.jobs = []

    def launch(self, steps):
        job = Job(steps)
        self.jobs.append(job)
        return job

    def turn(self, held, jobs=True):
        active = [job for job in self.jobs if jobs and job.active]
        flat = list(held)
        for job in active:
            flat.extend(job.waiting)
        if len(flat) > 1:
            flat = list(lax.optimization_barrier(tuple(flat)))
        begin = len(held)
        moved = []
        for job in active:
            moved.append(flat[begin : begin + len(job.waiting)])
            begin += len(job.waiting)
        return flat[: len(held)], list(zip(active, moved))

    def run(self, clips):
        under_way = None
        got = {}

        def settle(held, jobs=True):
            extra = [] if under_way is None else [under_way[1].sent, under_way[2]]
            out, moved = self.turn(held + extra, jobs)
            if under_way is not None:
                got[under_way[0]] = under_way[1].finish(out[-2], out[-1])
            for job, values in moved:
                job.advance(values)
            return out[: len(held)]

        queue = list(range(len(clips)))
        started = set()
        while queue:
            place = queue.pop(0)
            if under_way is not None and under_way[0] == place:
                settle([])
                under_way = None
            try:
                if place in started:
                    request = clips[place].send(got.pop(place))
                else:
                    started.add(place)
                    request = next(clips[place])
                while isinstance(request, Met):
                    values = settle(request.values, False)
                    under_way = None
                    request = clips[place].send(values)
            except StopIteration:
                continue
            (sent,) = settle([request.sent])
            request.sent = sent
            under_way = (place, request, request.move(sent))
            queue.append(place)

    def drain(self):
        while any(job.active for job in self.jobs):
            _, moved = self.turn([])
            for job, values in moved:
                job.advance(values)


def dp_grid():
    return lax.axis_size("dp") == 16


def dp_bit(bit):
    return (lax.axis_index("dp") // bit) % 2


def dp_swap(values, bit):
    return lax.ppermute(values, "dp", [(place, place ^ bit) for place in range(16)])


def piece_of(values, which, axis):
    return lax.dynamic_index_in_dim(values, which, axis, keepdims=False)


def add_low(left, right):
    return narrow(widen(left) + widen(right))


def unstack_columns(shards, values):
    width = shards.shape[-1]
    results = []
    begin = 0
    for value in values:
        size = value.shape[0] // shards.shape[0]
        pieces = []
        for _ in range(0, value.shape[1], width):
            pieces.append(shards[:, begin : begin + size].reshape(value.shape[0], width))
            begin += size
        results.append(jnp.concatenate(pieces, axis=1) if len(pieces) > 1 else pieces[0])
    return results


def split_rows(value):
    return value.reshape(2, 2, 2, 2, value.shape[0] // 16, value.shape[1])


def scatter_job(make, delay, width, eager):
    if not eager:
        yield []
    values = [narrow(value) for value in make()]
    if not dp_grid():
        return values, [lax.psum(value, "dp") for value in values]
    parts = []
    for value in values:
        for start in range(0, value.shape[1], width):
            parts.append(split_rows(value[:, start : start + width]))
    core, side, near, far = [dp_bit(bit) for bit in (1, 2, 4, 8)]
    sent = jnp.concatenate([piece_of(part, 1 - core, 3) for part in parts], axis=3)
    kept = jnp.concatenate([piece_of(part, core, 3) for part in parts], axis=3)
    part = add_low(kept, dp_swap(sent, 1))
    sent, kept = yield [piece_of(part, 1 - side, 2), piece_of(part, side, 2)]
    for _ in range(delay):
        yield []
    part = add_low(kept, dp_swap(sent, 2))
    sent, kept = yield [piece_of(part, 1 - near, 1), piece_of(part, near, 1)]
    part = add_low(kept, dp_swap(sent, 4))
    shard = add_low(piece_of(part, far, 0), dp_swap(piece_of(part, 1 - far, 0), 8))
    (shard,) = yield [shard]
    return values, shard


def sum_job(make):
    values = yield [narrow(value) for value in make()]
    summed = [lax.psum(value, "dp") for value in values]
    for _ in range(4):
        yield []
    return (yield summed)


def gather_job(jobs, turns):
    while any(job.active for job in jobs):
        yield []
    values = [value for job in jobs for value in job.result[0]]
    if not dp_grid():
        return [value for job in jobs for value in job.result[1]]
    shards = jnp.concatenate([job.result[1] for job in jobs], axis=0)
    whole = lax.all_gather(shards, "dp", axis=0)
    if turns is not None:
        for _ in range(turns):
            yield []
        (whole,) = yield [whole]
    return unstack_columns(whole, values)


def small_job(values):
    flat = jnp.concatenate([value.reshape(-1) for value in values])
    if dp_grid():
        for bit in (1, 2, 4, 8):
            (got,) = yield [dp_swap(flat, bit)]
            flat = flat + got
    else:
        flat = lax.psum(flat, "dp")
    results = []
    start = 0
    for value in values:
        results.append(flat[start : start + value.size].reshape(value.shape))
        start += value.size
    return results


SCALE = 1.0 / math.sqrt(HEAD_DIM)
PAIR = 2 * HEAD_DIM
QB = 128
WINDOW = 3 * QB
ROWS = 32


def keep_head(block, head):
    inside = lax.broadcasted_iota(jnp.int32, block.shape, 1) < HEAD_DIM
    if head == 1:
        inside = jnp.logical_not(inside)
    return jnp.where(inside, block, jnp.zeros_like(block))


def strip_place(begin, length):
    return (
        lax.broadcasted_iota(jnp.int32, (ROWS, length), 1)
        - lax.broadcasted_iota(jnp.int32, (ROWS, length), 0)
        - begin
    )


def strip_probs(content, relative, begin, place):
    length = content.shape[1]
    block = begin // QB
    low = max(block - 1, 0) * QB
    high = min(block + 2, length // QB) * QB
    before = relative[:, 0:1]
    after = relative[:, BACK + AHEAD : BACK + AHEAD + 1]
    turned = pltpu.roll(relative, (begin + QB - BACK) % QB, 1, stride=1, stride_axis=0)
    parts = []
    for start in range(0, length, QB):
        if start < low:
            parts.append(jnp.broadcast_to(before, (ROWS, QB)))
        elif start >= high:
            parts.append(jnp.broadcast_to(after, (ROWS, QB)))
        else:
            here = place[:, start : start + QB]
            parts.append(
                jnp.where(here < -BACK, before, jnp.where(here > AHEAD, after, turned))
            )
    scores = (content + jnp.concatenate(parts, axis=1)) * SCALE
    weights = jnp.exp(scores - jnp.max(scores, axis=-1, keepdims=True))
    return weights * (1.0 / jnp.sum(weights, axis=-1, keepdims=True))


def attend_kernel(query_ref, key_ref, value_ref, table_ref, context_ref, score_ref, probs_ref, band_ref):
    length = query_ref.shape[0]
    parts = []
    for head in range(2):
        query = keep_head(query_ref[...], head)
        score_ref[head] = product_right(query, key_ref[...])
        band_ref[head] = product(query, table_ref[...])
        for begin in range(0, length, ROWS):
            rows = slice(begin, begin + ROWS)
            probs_ref[head, rows] = narrow(
                strip_probs(
                    score_ref[head, rows],
                    band_ref[head, rows],
                    begin,
                    strip_place(begin, length),
                )
            )
        parts.append(product(probs_ref[head], value_ref[...]))
    lane = lax.broadcasted_iota(jnp.int32, parts[0].shape, 1)
    context_ref[...] = narrow(jnp.where(lane < HEAD_DIM, parts[0], parts[1]))


def gather_block(low_block, block, blocks, flip):
    low = max(block - 1, 0)
    high = min(block + 2, blocks)
    parts = []
    if block == 0:
        parts.append(jnp.zeros((QB, QB), jnp.bfloat16))
    parts.append(low_block[:, low * QB : high * QB])
    if block == blocks - 1:
        parts.append(jnp.zeros((QB, QB), jnp.bfloat16))
    reversed_rows = product(flip, jnp.concatenate(parts, axis=1))
    moved = pltpu.roll(
        reversed_rows, WINDOW - (QB - BACK) - (QB - 1), 1, stride=1, stride_axis=0
    )[:, :QB]
    return product(flip, narrow(moved))


def attend_back_kernel(
    query_ref,
    key_ref,
    value_ref,
    grad_ref,
    table_ref,
    rows_ref,
    query_grad_ref,
    key_grad_ref,
    value_grad_ref,
    query_sum_ref,
    value_sum_ref,
    table_grad_ref,
    score_ref,
    wide_ref,
    probs_ref,
    low_ref,
    band_ref,
    ends_ref,
):
    @pl.when(pl.program_id(0) == 0)
    def _():
        table_grad_ref[...] = jnp.zeros_like(table_grad_ref)

    length = query_ref.shape[0]
    blocks = length // QB
    query_turned = narrow(widen(query_ref[...]).T)
    grad_turned = narrow(widen(grad_ref[...]).T)
    flip = narrow(
        (
            lax.broadcasted_iota(jnp.int32, (QB, QB), 0)
            + lax.broadcasted_iota(jnp.int32, (QB, QB), 1)
            == QB - 1
        ).astype(jnp.float32)
    )
    lane = lax.broadcasted_iota(jnp.int32, (ROWS, QB), 1)
    query_parts = []
    key_parts = []
    value_parts = []
    for head in range(2):
        piece = slice(head * HEAD_DIM, (head + 1) * HEAD_DIM)
        query = keep_head(query_ref[...], head)
        score_ref[head] = product_right(query, key_ref[...])
        band_ref[head] = product(query, table_ref[...])
        wide_ref[head] = product_right(keep_head(grad_ref[...], head), value_ref[...])
        for begin in range(0, length, ROWS):
            rows = slice(begin, begin + ROWS)
            place = strip_place(begin, length)
            probs = strip_probs(score_ref[head, rows], band_ref[head, rows], begin, place)
            probs_ref[head, rows] = narrow(probs)
            probs_grad = wide_ref[head, rows]
            delta = jnp.sum(probs * probs_grad, axis=-1, keepdims=True)
            score_grad = narrow(probs * (probs_grad - delta))
            low_ref[head, rows] = score_grad
            wide = widen(score_grad)
            back = jnp.sum(jnp.where(place <= -BACK, wide, 0.0), axis=-1, keepdims=True)
            ahead = jnp.sum(jnp.where(place >= AHEAD, wide, 0.0), axis=-1, keepdims=True)
            ends_ref[head, rows] = jnp.where(
                lane == 0, back, jnp.where(lane == BACK + AHEAD, ahead, 0.0)
            )
        for block in range(blocks):
            rows = slice(block * QB, (block + 1) * QB)
            inner = gather_block(low_ref[head, rows], block, blocks, flip)
            column = lax.broadcasted_iota(jnp.int32, (QB, QB), 1)
            inside = jnp.logical_and(column > 0, column < BACK + AHEAD)
            band_ref[head, rows] = jnp.where(inside, inner, ends_ref[head, rows])
        value_parts.append(product(grad_turned[piece], probs_ref[head]))
        key_parts.append(product(query_turned[piece], low_ref[head]))
        band = band_ref[head]
        band_high = narrow(band)
        band_low = narrow(band - widen(band_high))
        query_parts.append(
            product(low_ref[head], key_ref[...])
            + product(band_high, rows_ref[...])
            + product(band_low, rows_ref[...])
        )
        table_grad_ref[...] += SCALE * (
            product(query_turned[piece], band_high) + product(query_turned[piece], band_low)
        )
    lane = lax.broadcasted_iota(jnp.int32, query_parts[0].shape, 1)
    query_grad = SCALE * jnp.where(lane < HEAD_DIM, query_parts[0], query_parts[1])
    query_grad_ref[...] = narrow(query_grad)
    query_sum_ref[...] = jnp.sum(query_grad, axis=0, keepdims=True)
    key_grad_ref[...] = narrow(SCALE * jnp.concatenate(key_parts, axis=0).T)
    value_grad = jnp.concatenate(value_parts, axis=0).T
    value_grad_ref[...] = narrow(value_grad)
    value_sum_ref[...] = jnp.sum(value_grad, axis=0, keepdims=True)


def pair_spec(length):
    return pl.BlockSpec((length, PAIR), lambda pair: (0, pair))


def fixed_spec(shape):
    return pl.BlockSpec(shape, lambda pair: tuple(0 for _ in shape))


def table_forms(relative_table):
    padded = jnp.pad(relative_table, ((0, QB - relative_table.shape[0]), (0, 0)))
    rows = jnp.concatenate([padded, padded], axis=1)
    return rows.T, rows


def attend_heads(query, keys, values, table):
    length, width = query.shape
    return pl.pallas_call(
        attend_kernel,
        out_shape=jax.ShapeDtypeStruct((length, width), jnp.bfloat16),
        grid=(width // PAIR,),
        in_specs=[pair_spec(length)] * 3 + [fixed_spec((PAIR, QB))],
        out_specs=pair_spec(length),
        scratch_shapes=[
            pltpu.VMEM((2, length, length), jnp.float32),
            pltpu.VMEM((2, length, length), jnp.bfloat16),
            pltpu.VMEM((2, length, QB), jnp.float32),
        ],
        compiler_params=pltpu.CompilerParams(vmem_limit_bytes=16 << 20),
        name="attend_heads",
    )(query, keys, values, table)


def attend_heads_back(query, keys, values, grad, table, rows):
    length, width = query.shape
    sums = pl.BlockSpec((1, PAIR), lambda pair: (0, pair))
    return pl.pallas_call(
        attend_back_kernel,
        out_shape=(
            jax.ShapeDtypeStruct((length, width), jnp.bfloat16),
            jax.ShapeDtypeStruct((length, width), jnp.bfloat16),
            jax.ShapeDtypeStruct((length, width), jnp.bfloat16),
            jax.ShapeDtypeStruct((1, width), jnp.float32),
            jax.ShapeDtypeStruct((1, width), jnp.float32),
            jax.ShapeDtypeStruct((HEAD_DIM, QB), jnp.float32),
        ),
        grid=(width // PAIR,),
        in_specs=[pair_spec(length)] * 4 + [fixed_spec((PAIR, QB)), fixed_spec((QB, PAIR))],
        out_specs=(pair_spec(length),) * 3 + (sums, sums, fixed_spec((HEAD_DIM, QB))),
        scratch_shapes=[
            pltpu.VMEM((2, length, length), jnp.float32),
            pltpu.VMEM((2, length, length), jnp.float32),
            pltpu.VMEM((2, length, length), jnp.bfloat16),
            pltpu.VMEM((2, length, length), jnp.bfloat16),
            pltpu.VMEM((2, length, QB), jnp.float32),
            pltpu.VMEM((2, length, QB), jnp.float32),
        ],
        compiler_params=pltpu.CompilerParams(vmem_limit_bytes=20 << 20),
        name="attend_heads_back",
    )(query, keys, values, grad, table, rows)
LANES = 128
STRIP = 64
EDGE = 32


def mix_kernel(linear_ref, gate_ref, taps_ref, mixed_ref, sums_ref, padded_ref, total_ref):
    length = linear_ref.shape[0]
    padded_ref[0:EDGE] = jnp.zeros((EDGE, LANES), jnp.float32)
    padded_ref[EDGE : EDGE + length] = linear_ref[...] * jax.nn.sigmoid(gate_ref[...])

    def strip(index, carry):
        begin = pl.multiple_of(index * STRIP, STRIP)
        total = jnp.zeros((STRIP, LANES), jnp.float32)
        for tap in range(CONV_K):
            total = total + padded_ref[
                pl.ds(begin + EDGE - CONV_K + 1 + tap, STRIP), :
            ] * taps_ref[tap : tap + 1, :]
        mixed_ref[pl.ds(begin, STRIP), :] = total
        return carry

    lax.fori_loop(0, length // STRIP, strip, 0)
    mixed = mixed_ref[...]

    @pl.when(pl.program_id(0) == 0)
    def _():
        total_ref[...] = jnp.zeros_like(total_ref)

    total_ref[0] += mixed
    total_ref[1] += mixed * mixed

    @pl.when(pl.program_id(0) == pl.num_programs(0) - 1)
    def _():
        ones = jnp.ones((8, LANES), jnp.float32)
        sums_ref[...] = jnp.concatenate(
            [
                lax.dot_general(
                    ones,
                    total_ref[place],
                    (((1,), (1,)), ((), ())),
                    precision=lax.Precision.HIGHEST,
                    preferred_element_type=jnp.float32,
                )
                for place in range(2)
            ],
            axis=0,
        )


def mix_channels(linear, gate, taps):
    length, width = linear.shape
    block = pl.BlockSpec((length, LANES), lambda part: (0, part))
    mixed, sums = pl.pallas_call(
        mix_kernel,
        out_shape=(
            jax.ShapeDtypeStruct((length, width), jnp.float32),
            jax.ShapeDtypeStruct((16, length), jnp.float32),
        ),
        grid=(width // LANES,),
        in_specs=[block, block, pl.BlockSpec((EDGE, LANES), lambda part: (0, part))],
        out_specs=(block, pl.BlockSpec((16, length), lambda part: (0, 0))),
        scratch_shapes=[
            pltpu.VMEM((EDGE + length, LANES), jnp.float32),
            pltpu.VMEM((2, length, LANES), jnp.float32),
        ],
        compiler_params=pltpu.CompilerParams(vmem_limit_bytes=8 << 20),
        name="mix_channels",
    )(linear, gate, taps)
    return mixed, jnp.concatenate([sums[0:1], sums[8:9]], axis=0)


def mix_back_kernel(
    grad_ref,
    linear_ref,
    gate_ref,
    taps_ref,
    linear_grad_ref,
    gating_grad_ref,
    taps_grad_ref,
    padded_ref,
    tail_ref,
    total_ref,
):
    length = linear_ref.shape[0]
    padded_ref[0:EDGE] = jnp.zeros((EDGE, LANES), jnp.float32)
    padded_ref[EDGE : EDGE + length] = linear_ref[...] * jax.nn.sigmoid(gate_ref[...])
    tail_ref[0:length] = grad_ref[...]
    tail_ref[length : length + EDGE] = jnp.zeros((EDGE, LANES), jnp.float32)
    total_ref[...] = jnp.zeros_like(total_ref)

    def strip(index, carry):
        begin = pl.multiple_of(index * STRIP, STRIP)
        here = pl.ds(begin, STRIP)
        grad = tail_ref[here, :]
        total = jnp.zeros((STRIP, LANES), jnp.float32)
        for tap in range(CONV_K):
            total = total + tail_ref[
                pl.ds(begin + CONV_K - 1 - tap, STRIP), :
            ] * taps_ref[tap : tap + 1, :]
            weighed = grad * padded_ref[pl.ds(begin + EDGE - CONV_K + 1 + tap, STRIP), :]
            total_ref[tap] += jnp.sum(weighed.reshape(STRIP // 8, 8, LANES), axis=0)
        sigma = jax.nn.sigmoid(gate_ref[here, :])
        low = total * sigma
        linear_grad_ref[here, :] = narrow(low)
        gating_grad_ref[here, :] = narrow(low * linear_ref[here, :] * (1.0 - sigma))
        return carry

    lax.fori_loop(0, length // STRIP, strip, 0)
    for tap in range(CONV_K):
        taps_grad_ref[tap : tap + 1, :] = jnp.sum(total_ref[tap], axis=0, keepdims=True)
    taps_grad_ref[CONV_K:EDGE, :] = jnp.zeros((EDGE - CONV_K, LANES), jnp.float32)


def mix_channels_back(grad, linear, gate, taps):
    length, width = linear.shape
    block = pl.BlockSpec((length, LANES), lambda part: (0, part))
    edge = pl.BlockSpec((EDGE, LANES), lambda part: (0, part))
    return pl.pallas_call(
        mix_back_kernel,
        out_shape=(
            jax.ShapeDtypeStruct((length, width), jnp.bfloat16),
            jax.ShapeDtypeStruct((length, width), jnp.bfloat16),
            jax.ShapeDtypeStruct((EDGE, width), jnp.float32),
        ),
        grid=(width // LANES,),
        in_specs=[block, block, block, edge],
        out_specs=(block, block, edge),
        scratch_shapes=[
            pltpu.VMEM((EDGE + length, LANES), jnp.float32),
            pltpu.VMEM((EDGE + length, LANES), jnp.float32),
            pltpu.VMEM((EDGE, 8, LANES), jnp.float32),
        ],
        compiler_params=pltpu.CompilerParams(vmem_limit_bytes=8 << 20),
        name="mix_channels_back",
    )(grad, linear, gate, taps)


def feed_forward(rows, gain, shift, up_weight, up_bias, down_weight):
    normed, center, inverse = layer_norm(rows, gain, shift)
    normed = narrow(normed)
    before = product(normed, up_weight) + up_bias
    hidden = narrow(before * jax.nn.sigmoid(before))
    return product(hidden, down_weight), (rows, center, inverse, normed, before, hidden)


def feed_back(incoming, kept, up_weight, down_weight):
    before = kept[4]
    branch_grad = 0.5 * incoming
    spread = narrow(branch_grad)
    sigma = jax.nn.sigmoid(before)
    before_grad = product_right(spread, down_weight) * sigma * (1.0 + before * (1.0 - sigma))
    before_low = narrow(before_grad)
    share = product_right(before_low, up_weight)
    return share, spread, before_low, jnp.sum(before_grad, axis=0), jnp.sum(branch_grad, axis=0)


def residual_back(incoming, normed_grad, kept, gain):
    rows, center, inverse = kept[:3]
    normal = (rows - center) * inverse
    result, gain_grad, shift_grad = norm_back(normed_grad, normal, inverse, gain)
    return incoming + result, gain_grad, shift_grad


def attend(
    rows, gain, shift, query_weight, query_bias, key_weight, value_weight, value_bias, output_weight, table
):
    normed, center, inverse = layer_norm(rows, gain, shift)
    normed = narrow(normed)
    query = narrow(product(normed, query_weight) + query_bias)
    keys = narrow(product(normed, key_weight))
    values = narrow(product(normed, value_weight) + value_bias)
    context = attend_heads(query, keys, values, table)
    return (
        product(context, output_weight),
        (rows, center, inverse, normed, query, keys, values, context),
    )


def attend_back(
    incoming, kept, query_weight, key_weight, value_weight, output_weight, table, table_rows
):
    query, keys, values = kept[4:7]
    spread = narrow(incoming)
    context_grad = narrow(product_right(spread, output_weight))
    query_low, key_low, value_low, query_sum, value_sum, table_grad = attend_heads_back(
        query, keys, values, context_grad, table, table_rows
    )
    query_low, key_low, value_low = yield Met([query_low, key_low, value_low])
    share = (
        product_right(query_low, query_weight)
        + product_right(key_low, key_weight)
        + product_right(value_low, value_weight)
    )
    return (
        share,
        spread,
        (query_low, key_low, value_low),
        query_sum[0],
        value_sum[0],
        jnp.sum(incoming, axis=0),
        table_grad,
    )


def mix(rows, gain, shift, pointwise_in, taps):
    normed, center, inverse = layer_norm(rows, gain, shift)
    normed = narrow(normed)
    linear = product(normed, pointwise_in[0])
    gate = product(normed, pointwise_in[1])
    mixed, sums = yield Met(mix_channels(linear, gate, taps))
    return mixed, wide_sum(sums), (rows, center, inverse, normed, linear, gate)


def convolve(mixed, sums, depth_gain, depth_shift, pointwise_out):
    center = (sums[0] / D)[:, None]
    channel_inverse = lax.rsqrt(sums[1][:, None] / D - center * center + epsilon)
    channel_normal = (mixed - center) * channel_inverse
    shaped = channel_normal * depth_gain + depth_shift
    active = narrow(shaped * jax.nn.sigmoid(shaped))
    return product(active, pointwise_out), (channel_inverse, channel_normal, shaped, active)


def shape_back(incoming, shape_kept, depth_gain, pointwise_out):
    channel_inverse, channel_normal, shaped, active = shape_kept
    spread = narrow(incoming)
    sigma = jax.nn.sigmoid(shaped)
    shaped_grad = product_right(spread, pointwise_out) * sigma * (1.0 + shaped * (1.0 - sigma))
    scaled = shaped_grad * depth_gain
    sums = wide_sum(
        jnp.stack([jnp.sum(scaled, axis=-1), jnp.sum(scaled * channel_normal, axis=-1)])
    )
    return (
        spread,
        scaled,
        sums,
        jnp.sum(shaped_grad * channel_normal, axis=0),
        jnp.sum(shaped_grad, axis=0),
    )


def convolve_back(scaled, sums, kept, shape_kept, pointwise_in, taps):
    linear, gate = kept[4:6]
    channel_inverse, channel_normal = shape_kept[:2]
    mixed_grad = channel_inverse * (
        scaled - (sums[0] / D)[:, None] - channel_normal * (sums[1] / D)[:, None]
    )
    linear_low, gating_low, taps_grad = mix_channels_back(mixed_grad, linear, gate, taps)
    share = product_right(linear_low, pointwise_in[0]) + product_right(gating_low, pointwise_in[1])
    return share, linear_low, gating_low, taps_grad[:CONV_K]


def total(parts):
    result = parts[0]
    for part in parts[1:]:
        result = result + part
    return result


def weight_grad_kernel(count, *refs):
    total = product_left(refs[0][...], refs[1][...])
    for place in range(1, count):
        total = total + product_left(refs[2 * place][...], refs[2 * place + 1][...])
    refs[2 * count][...] = narrow(total)


def tile_of(size, limit):
    tile = size
    while tile > limit:
        tile //= 2
    return tile


def weight_grad(lefts, rights):
    length, rows = lefts[0].shape
    columns = rights[0].shape[1]
    row_tile, column_tile = tile_of(rows, 1024), tile_of(columns, 1024)
    operands = [value for pair in zip(lefts, rights) for value in pair]
    return pl.pallas_call(
        functools.partial(weight_grad_kernel, len(lefts)),
        out_shape=jax.ShapeDtypeStruct((rows, columns), jnp.bfloat16),
        grid=(rows // row_tile, columns // column_tile),
        in_specs=[
            pl.BlockSpec((length, row_tile), lambda row, column: (0, row)),
            pl.BlockSpec((length, column_tile), lambda row, column: (0, column)),
        ]
        * len(lefts),
        out_specs=pl.BlockSpec((row_tile, column_tile), lambda row, column: (row, column)),
        compiler_params=pltpu.CompilerParams(vmem_limit_bytes=24 << 20),
        name="weight_grad",
    )(*operands)


class Gradients:
    def __init__(self, flow, count):
        self.flow = flow
        self.count = count
        self.parts = {}
        self.jobs = {}

    def add(self, name, part):
        parts = self.parts.setdefault(name, [])
        parts.append(part)
        return len(parts) == self.count

    def maker(self, name):
        parts = self.parts[name]
        return lambda: [
            weight_grad([part[place][0] for part in parts], [part[place][1] for part in parts])
            for place in range(len(parts[0]))
        ]

    def weights(self, name, pairs, width, delay=0, eager=False):
        if self.add(name, pairs):
            self.jobs[name] = self.flow.launch(scatter_job(self.maker(name), delay, width, eager))

    def sums(self, name, values):
        self.add(name, values)

    def reduce_sums(self, name, groups):
        values = []
        for group in groups:
            parts = self.parts[group]
            values.extend(total([part[place] for part in parts]) for place in range(len(parts[0])))
        self.jobs[name] = self.flow.launch(small_job(values))

    def whole(self, name, pairs):
        if self.add(name, pairs):
            self.jobs[name] = self.flow.launch(sum_job(self.maker(name)))

    def gather(self, name, members, turns=None):
        if members[-1] in self.jobs and name not in self.jobs:
            self.jobs[name] = self.flow.launch(
                gather_job([self.jobs[member] for member in members], turns)
            )

    def result(self, name):
        return self.jobs[name].result


def per_device(
    tokens,
    clip_count,
    first_norm_gain,
    first_norm_shift,
    first_up_weight,
    first_up_bias,
    first_down_weight,
    first_down_bias,
    attend_norm_gain,
    attend_norm_shift,
    query_weight,
    query_bias,
    key_weight,
    value_weight,
    value_bias,
    output_weight,
    output_bias,
    relative_table,
    convolve_norm_gain,
    convolve_norm_shift,
    pointwise_in,
    depthwise_weight,
    depth_norm_gain,
    depth_norm_shift,
    pointwise_out,
    second_norm_gain,
    second_norm_shift,
    second_up_weight,
    second_up_bias,
    second_down_weight,
    second_down_bias,
    final_norm_gain,
    final_norm_shift,
    cotangent,
):
    slots = range(tokens.shape[0])
    live_count = clip_count[0]
    first_gain = widen(first_norm_gain)
    attend_gain = widen(attend_norm_gain)
    convolve_gain = widen(convolve_norm_gain)
    second_gain = widen(second_norm_gain)
    final_gain = widen(final_norm_gain)
    taps = jnp.pad(widen(depthwise_weight), ((0, EDGE - CONV_K), (0, 0)))
    depth_gain = widen(depth_norm_gain)
    table, table_rows = table_forms(relative_table)
    flow = Flow()
    grads = Gradients(flow, len(slots))
    outputs = {}
    input_grads = {}
    count_job = flow.launch(small_job([jnp.full((1, 128), widen(live_count), jnp.float32)]))

    def clip(slot):
        live = (live_count > slot).astype(jnp.float32)
        rows = widen((yield Gathered(tokens[slot])))
        share, first_kept = feed_forward(
            rows,
            first_gain,
            widen(first_norm_shift),
            first_up_weight,
            widen(first_up_bias),
            first_down_weight,
        )
        rows = rows + 0.5 * ((yield Summed(share)) + widen(first_down_bias))
        share, attend_kept = attend(
            rows,
            attend_gain,
            widen(attend_norm_shift),
            query_weight,
            widen(query_bias),
            key_weight,
            value_weight,
            widen(value_bias),
            output_weight,
            table,
        )
        rows = rows + (yield Summed(share)) + widen(output_bias)
        mixed, sums, convolve_kept = yield from mix(
            rows, convolve_gain, widen(convolve_norm_shift), pointwise_in, taps
        )
        share, shape_kept = convolve(
            mixed, sums, depth_gain, widen(depth_norm_shift), pointwise_out
        )
        rows = rows + (yield Summed(share))
        share, second_kept = feed_forward(
            rows,
            second_gain,
            widen(second_norm_shift),
            second_up_weight,
            widen(second_up_bias),
            second_down_weight,
        )
        last = own_rows(rows) + 0.5 * ((yield Scattered(share)) + widen(second_down_bias))
        normed, center, inverse = layer_norm(last, final_gain, widen(final_norm_shift))
        outputs[slot] = narrow(normed * live)
        grad, gain_grad, shift_grad = norm_back(
            widen(cotangent[slot]) * live, (last - center) * inverse, inverse, final_gain
        )
        grads.sums("final", [gain_grad, shift_grad])

        grad = widen((yield Gathered(narrow(grad))))
        share, spread, before_low, up_sum, down_sum = feed_back(
            grad, second_kept, second_up_weight, second_down_weight
        )
        grads.whole("second_both", [(second_kept[5], spread), (second_kept[3], before_low)])
        normed_grad = yield Summed(share)
        grad, gain_grad, shift_grad = residual_back(grad, normed_grad, second_kept, second_gain)
        grads.sums("second", [up_sum, down_sum, gain_grad, shift_grad])

        spread, scaled, sums, depth_gain_sum, depth_shift_sum = shape_back(
            grad, shape_kept, depth_gain, pointwise_out
        )
        share, linear_low, gating_low, depthwise_sum = convolve_back(
            scaled, sums, convolve_kept, shape_kept, pointwise_in, taps
        )
        grads.weights(
            "convolve",
            [
                (convolve_kept[3], linear_low),
                (convolve_kept[3], gating_low),
                (shape_kept[3], spread),
            ],
            linear_low.shape[1],
        )
        normed_grad = yield Summed(share)
        grad, gain_grad, shift_grad = residual_back(
            grad, normed_grad, convolve_kept, convolve_gain
        )
        grads.sums(
            "convolve_sums", [depth_gain_sum, depth_shift_sum, depthwise_sum, gain_grad, shift_grad]
        )

        share, spread, lows, query_sum, value_sum, output_sum, table_sum = yield from attend_back(
            grad,
            attend_kept,
            query_weight,
            key_weight,
            value_weight,
            output_weight,
            table,
            table_rows,
        )
        grads.weights(
            "attend",
            [(attend_kept[7], spread)] + [(attend_kept[3], low) for low in lows],
            lows[0].shape[1],
        )
        grads.sums("attend_sums", [query_sum, value_sum, output_sum, table_sum])
        if slot == slots[-1]:
            grads.parts["final"] = [
                list(wide_sum(total([jnp.stack(part) for part in grads.parts["final"]])))
            ]
            grads.reduce_sums("early", ["final", "second", "convolve_sums", "attend_sums"])
        grads.gather("middle", ["convolve", "attend"])
        normed_grad = yield Summed(share)
        grad, gain_grad, shift_grad = residual_back(grad, normed_grad, attend_kept, attend_gain)
        grads.sums("attend_norm", [gain_grad, shift_grad])

        share, spread, before_low, up_sum, down_sum = feed_back(
            grad, first_kept, first_up_weight, first_down_weight
        )
        grads.weights("first_down", [(first_kept[5], spread)], spread.shape[1], eager=True)
        grads.weights("first_up", [(first_kept[3], before_low)], spread.shape[1], 1, eager=True)
        grads.gather("first_both", ["first_down", "first_up"])
        normed_grad = yield Scattered(share)
        input_grads[slot], gain_grad, shift_grad = residual_back(
            own_rows(grad),
            normed_grad,
            [own_rows(kept) for kept in first_kept[:3]],
            first_gain,
        )
        grads.sums("first", [up_sum, down_sum])
        grads.sums("first_norm", [gain_grad, shift_grad])

    flow.run([clip(slot) for slot in slots])
    grads.parts["first_norm"] = [
        list(wide_sum(total([jnp.stack(part) for part in grads.parts["first_norm"]])))
    ]
    grads.reduce_sums("late", ["attend_norm", "first", "first_norm"])
    flow.drain()

    clips = count_job.result[0][0, 0]
    early = grads.result("early")
    late = grads.result("late")
    second_down, second_up = grads.result("second_both")
    linear, gating, point_out, output_grad, query_grad, key_grad, value_grad = grads.result("middle")
    first_down, first_up = grads.result("first_both")
    table_grad = wide_sum(early[14]).T[: relative_table.shape[0]]
    every = (
        late[4],
        late[5],
        first_up,
        late[2],
        first_down,
        late[3],
        late[0],
        late[1],
        query_grad,
        early[11],
        key_grad,
        value_grad,
        early[12],
        output_grad,
        early[13],
        table_grad,
        early[9],
        early[10],
        jnp.stack([linear, gating]),
        early[8],
        early[6],
        early[7],
        point_out,
        early[4],
        early[5],
        second_up,
        early[2],
        second_down,
        early[3],
        early[0],
        early[1],
    )
    return (
        jnp.stack([outputs[slot] for slot in slots]),
        jnp.stack([input_grads[slot] for slot in slots]),
    ) + tuple(widen(value) / clips for value in every)


def solution(mesh):
    placed = (
        P("dp", "tensor", None),
        P("dp"),
        P(),
        P(),
        P(None, "tensor"),
        P("tensor"),
        P("tensor", None),
        P(),
        P(),
        P(),
        P(None, "tensor"),
        P("tensor"),
        P(None, "tensor"),
        P(None, "tensor"),
        P("tensor"),
        P("tensor", None),
        P(),
        P(),
        P(),
        P(),
        P(None, None, "tensor"),
        P(None, "tensor"),
        P("tensor"),
        P("tensor"),
        P("tensor", None),
        P(),
        P(),
        P(None, "tensor"),
        P("tensor"),
        P("tensor", None),
        P(),
        P(),
        P(),
        P("dp", "tensor", None),
    )
    return jax.shard_map(
        per_device,
        mesh=mesh,
        in_specs=placed,
        out_specs=(
            P("dp", "tensor", None),
            P("dp", "tensor", None),
            P(),
            P(),
            P(None, "tensor"),
            P("tensor"),
            P("tensor", None),
            P(),
            P(),
            P(),
            P(None, "tensor"),
            P("tensor"),
            P(None, "tensor"),
            P(None, "tensor"),
            P("tensor"),
            P("tensor", None),
            P(),
            P(),
            P(),
            P(),
            P(None, None, "tensor"),
            P(None, "tensor"),
            P("tensor"),
            P("tensor"),
            P("tensor", None),
            P(),
            P(),
            P(None, "tensor"),
            P("tensor"),
            P("tensor", None),
            P(),
            P(),
            P(),
        ),
        check_vma=False,
    )
```

```python
import functools
import math

import jax
import jax.numpy as jnp
from jax import lax
from jax.experimental import pallas as pl
from jax.experimental.pallas import tpu as pltpu
from jax.sharding import PartitionSpec as P

D = 1024
HEAD_DIM = 64
CONV_K = 31
BACK = 64
AHEAD = 8

epsilon = 1e-05


def product(left, right):
    return jnp.dot(left, right, preferred_element_type=jnp.float32)


def product_left(left, right):
    return lax.dot_general(
        left, right, (((0,), (0,)), ((), ())), preferred_element_type=jnp.float32
    )


def product_right(left, right):
    return lax.dot_general(
        left, right, (((1,), (1,)), ((), ())), preferred_element_type=jnp.float32
    )


def widen(value):
    return value.astype(jnp.float32)


def narrow(value):
    return value.astype(jnp.bfloat16)


def norm_stats(values):
    center = jnp.mean(values, axis=-1, keepdims=True)
    offset = values - center
    inverse = lax.rsqrt(jnp.mean(offset * offset, axis=-1, keepdims=True) + epsilon)
    return center, inverse


def layer_norm(values, gain, shift):
    center, inverse = norm_stats(values)
    normal = (values - center) * inverse
    return normal * gain + shift, center, inverse


def norm_back(incoming, normal, inverse, gain):
    scaled = incoming * gain
    first_mean = jnp.mean(scaled, axis=-1, keepdims=True)
    second_mean = jnp.mean(scaled * normal, axis=-1, keepdims=True)
    result = inverse * (scaled - first_mean - normal * second_mean)
    return (result, jnp.sum(incoming * normal, axis=0), jnp.sum(incoming, axis=0))


def paired():
    return lax.axis_size("tensor") == 2


def swap(values):
    return lax.ppermute(values, "tensor", [(0, 1), (1, 0)])


def rows_of(values, which):
    count = values.shape[0] // lax.axis_size("tensor")
    return lax.dynamic_slice_in_dim(values, which * count, count, 0)


def own_rows(values):
    return rows_of(values, lax.axis_index("tensor"))


def wide_sum(share):
    if paired():
        count = 2 * lax.axis_size("dp")
        pairs = [(place, place ^ 1) for place in reversed(range(count))]
        return share + lax.ppermute(share, ("dp", "tensor"), pairs)
    return lax.psum(share, "tensor")


class Gathered:
    def __init__(self, values):
        self.sent = values

    def move(self, sent):
        if paired():
            return swap(sent)
        return lax.all_gather(sent, "tensor", axis=0, tiled=True)

    def finish(self, sent, got):
        if not paired():
            return got
        first = lax.axis_index("tensor") == 0
        return jnp.concatenate(
            [jnp.where(first, sent, got), jnp.where(first, got, sent)], axis=0
        )


class Summed:
    def __init__(self, share):
        self.sent = narrow(share)

    def move(self, sent):
        if paired():
            return swap(sent)
        return lax.psum(sent, "tensor")

    def finish(self, sent, got):
        if not paired():
            return widen(got)
        return widen(sent) + widen(got)


class Scattered:
    def __init__(self, share):
        self.own = None
        if paired():
            self.own = own_rows(share)
            self.sent = narrow(rows_of(share, 1 - lax.axis_index("tensor")))
        else:
            self.sent = narrow(share)

    def move(self, sent):
        if paired():
            return swap(sent)
        return lax.psum_scatter(sent, "tensor", scatter_dimension=0, tiled=True)

    def finish(self, sent, got):
        if self.own is None:
            return widen(got)
        return self.own + widen(got)


class Met:
    def __init__(self, values):
        self.values = list(values)


class Job:
    def __init__(self, steps):
        self.steps = steps
        self.result = None
        self.waiting = []
        self.active = True
        self.advance(None)

    def advance(self, values):
        try:
            self.waiting = list(self.steps.send(values))
        except StopIteration as ended:
            self.active = False
            self.waiting = []
            self.result = ended.value


class Flow:
    def __init__(self):
        self.jobs = []

    def launch(self, steps):
        job = Job(steps)
        self.jobs.append(job)
        return job

    def turn(self, held, jobs=True):
        active = [job for job in self.jobs if jobs and job.active]
        flat = list(held)
        for job in active:
            flat.extend(job.waiting)
        if len(flat) > 1:
            flat = list(lax.optimization_barrier(tuple(flat)))
        begin = len(held)
        moved = []
        for job in active:
            moved.append(flat[begin : begin + len(job.waiting)])
            begin += len(job.waiting)
        return flat[: len(held)], list(zip(active, moved))

    def run(self, clips):
        under_way = None
        arrived = {}

        def settle(held, jobs=True):
            extra = [] if under_way is None else [under_way[1].sent, under_way[2]]
            if under_way is not None:
                arrived[under_way[0]] = (under_way[1], *extra)
            waiting = list(arrived)
            extra = [value for place in waiting for value in arrived[place][1:]]
            out, moved = self.turn(held + extra, jobs)
            for index, place in enumerate(waiting):
                begin = len(held) + 2 * index
                arrived[place] = (arrived[place][0], *out[begin : begin + 2])
            for job, values in moved:
                job.advance(values)
            return out[: len(held)]

        queue = list(range(len(clips)))
        started = set()
        while queue:
            place = queue.pop(0)
            if under_way is not None and under_way[0] == place:
                settle([])
                under_way = None
            try:
                if place in started:
                    earlier, sent, got = arrived.pop(place)
                    request = clips[place].send(earlier.finish(sent, got))
                else:
                    started.add(place)
                    request = next(clips[place])
                while isinstance(request, Met):
                    values = settle(request.values, False)
                    under_way = None
                    request = clips[place].send(values)
            except StopIteration:
                continue
            (sent,) = settle([request.sent])
            request.sent = sent
            under_way = (place, request, request.move(sent))
            queue.append(place)

    def drain(self):
        while any(job.active for job in self.jobs):
            _, moved = self.turn([])
            for job, values in moved:
                job.advance(values)


def dp_grid():
    return lax.axis_size("dp") == 16


def dp_bit(bit):
    return (lax.axis_index("dp") // bit) % 2


def dp_swap(values, bit):
    return lax.ppermute(values, "dp", [(place, place ^ bit) for place in range(16)])


def piece_of(values, which, axis):
    return lax.dynamic_index_in_dim(values, which, axis, keepdims=False)


def add_low(left, right):
    return narrow(widen(left) + widen(right))


def unstack_columns(shards, values):
    width = shards.shape[-1]
    results = []
    begin = 0
    for value in values:
        size = value.shape[0] // shards.shape[0]
        pieces = []
        for _ in range(0, value.shape[1], width):
            pieces.append(shards[:, begin : begin + size].reshape(value.shape[0], width))
            begin += size
        results.append(jnp.concatenate(pieces, axis=1) if len(pieces) > 1 else pieces[0])
    return results


def split_rows(value):
    return value.reshape(2, 2, 2, 2, value.shape[0] // 16, value.shape[1])


def scatter_job(make, delay, width, eager):
    if not eager:
        yield []
    values = [narrow(value) for value in make()]
    if not dp_grid():
        return values, [lax.psum(value, "dp") for value in values]
    parts = []
    for value in values:
        for start in range(0, value.shape[1], width):
            parts.append(split_rows(value[:, start : start + width]))
    core, side, near, far = [dp_bit(bit) for bit in (1, 2, 4, 8)]
    sent = jnp.concatenate([piece_of(part, 1 - core, 3) for part in parts], axis=3)
    kept = jnp.concatenate([piece_of(part, core, 3) for part in parts], axis=3)
    part = add_low(kept, dp_swap(sent, 1))
    sent, kept = yield [piece_of(part, 1 - side, 2), piece_of(part, side, 2)]
    for _ in range(delay):
        yield []
    part = add_low(kept, dp_swap(sent, 2))
    sent, kept = yield [piece_of(part, 1 - near, 1), piece_of(part, near, 1)]
    part = add_low(kept, dp_swap(sent, 4))
    shard = add_low(piece_of(part, far, 0), dp_swap(piece_of(part, 1 - far, 0), 8))
    (shard,) = yield [shard]
    return values, shard


def sum_job(make):
    values = yield [narrow(value) for value in make()]
    summed = [lax.psum(value, "dp") for value in values]
    for _ in range(5):
        yield []
    return (yield summed)


def gather_job(jobs, turns):
    while any(job.active for job in jobs):
        yield []
    values = [value for job in jobs for value in job.result[0]]
    if not dp_grid():
        return [value for job in jobs for value in job.result[1]]
    shards = jnp.concatenate([job.result[1] for job in jobs], axis=0)
    whole = lax.all_gather(shards, "dp", axis=0)
    if turns is not None:
        for _ in range(turns):
            yield []
        (whole,) = yield [whole]
    return unstack_columns(whole, values)


def small_job(values):
    flat = jnp.concatenate([value.reshape(-1) for value in values])
    if dp_grid():
        for bit in (1, 2, 4, 8):
            (got,) = yield [dp_swap(flat, bit)]
            flat = flat + got
    else:
        flat = lax.psum(flat, "dp")
    results = []
    start = 0
    for value in values:
        results.append(flat[start : start + value.size].reshape(value.shape))
        start += value.size
    return results


SCALE = 1.0 / math.sqrt(HEAD_DIM)
PAIR = 2 * HEAD_DIM
QB = 128
WINDOW = 3 * QB
ROWS = 32


def keep_head(block, head):
    inside = lax.broadcasted_iota(jnp.int32, block.shape, 1) < HEAD_DIM
    if head == 1:
        inside = jnp.logical_not(inside)
    return jnp.where(inside, block, jnp.zeros_like(block))


def strip_place(begin, length):
    return (
        lax.broadcasted_iota(jnp.int32, (ROWS, length), 1)
        - lax.broadcasted_iota(jnp.int32, (ROWS, length), 0)
        - begin
    )


def strip_probs(content, relative, begin, place):
    length = content.shape[1]
    block = begin // QB
    low = max(block - 1, 0) * QB
    high = min(block + 2, length // QB) * QB
    before = relative[:, 0:1]
    after = relative[:, BACK + AHEAD : BACK + AHEAD + 1]
    turned = pltpu.roll(relative, (begin + QB - BACK) % QB, 1, stride=1, stride_axis=0)
    parts = []
    for start in range(0, length, QB):
        if start < low:
            parts.append(jnp.broadcast_to(before, (ROWS, QB)))
        elif start >= high:
            parts.append(jnp.broadcast_to(after, (ROWS, QB)))
        else:
            here = place[:, start : start + QB]
            parts.append(
                jnp.where(here < -BACK, before, jnp.where(here > AHEAD, after, turned))
            )
    scores = (content + jnp.concatenate(parts, axis=1)) * SCALE
    weights = jnp.exp(scores - jnp.max(scores, axis=-1, keepdims=True))
    return weights * (1.0 / jnp.sum(weights, axis=-1, keepdims=True))


def attend_kernel(query_ref, key_ref, value_ref, table_ref, context_ref, score_ref, probs_ref, band_ref):
    length = query_ref.shape[0]
    parts = []
    for head in range(2):
        query = keep_head(query_ref[...], head)
        score_ref[head] = product_right(query, key_ref[...])
        band_ref[head] = product(query, table_ref[...])
        for begin in range(0, length, ROWS):
            rows = slice(begin, begin + ROWS)
            probs_ref[head, rows] = narrow(
                strip_probs(
                    score_ref[head, rows],
                    band_ref[head, rows],
                    begin,
                    strip_place(begin, length),
                )
            )
        parts.append(product(probs_ref[head], value_ref[...]))
    lane = lax.broadcasted_iota(jnp.int32, parts[0].shape, 1)
    context_ref[...] = narrow(jnp.where(lane < HEAD_DIM, parts[0], parts[1]))


def gather_block(low_block, block, blocks, flip):
    low = max(block - 1, 0)
    high = min(block + 2, blocks)
    parts = []
    if block == 0:
        parts.append(jnp.zeros((QB, QB), jnp.bfloat16))
    parts.append(low_block[:, low * QB : high * QB])
    if block == blocks - 1:
        parts.append(jnp.zeros((QB, QB), jnp.bfloat16))
    reversed_rows = product(flip, jnp.concatenate(parts, axis=1))
    moved = pltpu.roll(
        reversed_rows, WINDOW - (QB - BACK) - (QB - 1), 1, stride=1, stride_axis=0
    )[:, :QB]
    return product(flip, narrow(moved))


def attend_back_kernel(
    query_ref,
    key_ref,
    value_ref,
    grad_ref,
    table_ref,
    rows_ref,
    query_grad_ref,
    key_grad_ref,
    value_grad_ref,
    query_sum_ref,
    value_sum_ref,
    table_grad_ref,
    score_ref,
    wide_ref,
    probs_ref,
    low_ref,
    band_ref,
    ends_ref,
):
    @pl.when(pl.program_id(0) == 0)
    def _():
        table_grad_ref[...] = jnp.zeros_like(table_grad_ref)

    length = query_ref.shape[0]
    blocks = length // QB
    query_turned = narrow(widen(query_ref[...]).T)
    grad_turned = narrow(widen(grad_ref[...]).T)
    flip = narrow(
        (
            lax.broadcasted_iota(jnp.int32, (QB, QB), 0)
            + lax.broadcasted_iota(jnp.int32, (QB, QB), 1)
            == QB - 1
        ).astype(jnp.float32)
    )
    lane = lax.broadcasted_iota(jnp.int32, (ROWS, QB), 1)
    query_parts = []
    key_parts = []
    value_parts = []
    for head in range(2):
        piece = slice(head * HEAD_DIM, (head + 1) * HEAD_DIM)
        query = keep_head(query_ref[...], head)
        score_ref[head] = product_right(query, key_ref[...])
        band_ref[head] = product(query, table_ref[...])
        wide_ref[head] = product_right(keep_head(grad_ref[...], head), value_ref[...])
        for begin in range(0, length, ROWS):
            rows = slice(begin, begin + ROWS)
            place = strip_place(begin, length)
            probs = strip_probs(score_ref[head, rows], band_ref[head, rows], begin, place)
            probs_ref[head, rows] = narrow(probs)
            probs_grad = wide_ref[head, rows]
            delta = jnp.sum(probs * probs_grad, axis=-1, keepdims=True)
            score_grad = narrow(probs * (probs_grad - delta))
            low_ref[head, rows] = score_grad
            wide = widen(score_grad)
            back = jnp.sum(jnp.where(place <= -BACK, wide, 0.0), axis=-1, keepdims=True)
            ahead = jnp.sum(jnp.where(place >= AHEAD, wide, 0.0), axis=-1, keepdims=True)
            ends_ref[head, rows] = jnp.where(
                lane == 0, back, jnp.where(lane == BACK + AHEAD, ahead, 0.0)
            )
        for block in range(blocks):
            rows = slice(block * QB, (block + 1) * QB)
            inner = gather_block(low_ref[head, rows], block, blocks, flip)
            column = lax.broadcasted_iota(jnp.int32, (QB, QB), 1)
            inside = jnp.logical_and(column > 0, column < BACK + AHEAD)
            band_ref[head, rows] = jnp.where(inside, inner, ends_ref[head, rows])
        value_parts.append(product(grad_turned[piece], probs_ref[head]))
        key_parts.append(product(query_turned[piece], low_ref[head]))
        band = band_ref[head]
        band_high = narrow(band)
        band_low = narrow(band - widen(band_high))
        query_parts.append(
            product(low_ref[head], key_ref[...])
            + product(band_high, rows_ref[...])
            + product(band_low, rows_ref[...])
        )
        table_grad_ref[...] += SCALE * (
            product(query_turned[piece], band_high) + product(query_turned[piece], band_low)
        )
    lane = lax.broadcasted_iota(jnp.int32, query_parts[0].shape, 1)
    query_grad = SCALE * jnp.where(lane < HEAD_DIM, query_parts[0], query_parts[1])
    query_grad_ref[...] = narrow(query_grad)
    query_sum_ref[...] = jnp.sum(query_grad, axis=0, keepdims=True)
    key_grad_ref[...] = narrow(SCALE * jnp.concatenate(key_parts, axis=0).T)
    value_grad = jnp.concatenate(value_parts, axis=0).T
    value_grad_ref[...] = narrow(value_grad)
    value_sum_ref[...] = jnp.sum(value_grad, axis=0, keepdims=True)


def pair_spec(length):
    return pl.BlockSpec((length, PAIR), lambda pair: (0, pair))


def fixed_spec(shape):
    return pl.BlockSpec(shape, lambda pair: tuple(0 for _ in shape))


def table_forms(relative_table):
    padded = jnp.pad(relative_table, ((0, QB - relative_table.shape[0]), (0, 0)))
    rows = jnp.concatenate([padded, padded], axis=1)
    return rows.T, rows


def attend_heads(query, keys, values, table):
    length, width = query.shape
    return pl.pallas_call(
        attend_kernel,
        out_shape=jax.ShapeDtypeStruct((length, width), jnp.bfloat16),
        grid=(width // PAIR,),
        in_specs=[pair_spec(length)] * 3 + [fixed_spec((PAIR, QB))],
        out_specs=pair_spec(length),
        scratch_shapes=[
            pltpu.VMEM((2, length, length), jnp.float32),
            pltpu.VMEM((2, length, length), jnp.bfloat16),
            pltpu.VMEM((2, length, QB), jnp.float32),
        ],
        compiler_params=pltpu.CompilerParams(vmem_limit_bytes=16 << 20),
        name="attend_heads",
    )(query, keys, values, table)


def attend_heads_back(query, keys, values, grad, table, rows):
    length, width = query.shape
    sums = pl.BlockSpec((1, PAIR), lambda pair: (0, pair))
    return pl.pallas_call(
        attend_back_kernel,
        out_shape=(
            jax.ShapeDtypeStruct((length, width), jnp.bfloat16),
            jax.ShapeDtypeStruct((length, width), jnp.bfloat16),
            jax.ShapeDtypeStruct((length, width), jnp.bfloat16),
            jax.ShapeDtypeStruct((1, width), jnp.float32),
            jax.ShapeDtypeStruct((1, width), jnp.float32),
            jax.ShapeDtypeStruct((HEAD_DIM, QB), jnp.float32),
        ),
        grid=(width // PAIR,),
        in_specs=[pair_spec(length)] * 4 + [fixed_spec((PAIR, QB)), fixed_spec((QB, PAIR))],
        out_specs=(pair_spec(length),) * 3 + (sums, sums, fixed_spec((HEAD_DIM, QB))),
        scratch_shapes=[
            pltpu.VMEM((2, length, length), jnp.float32),
            pltpu.VMEM((2, length, length), jnp.float32),
            pltpu.VMEM((2, length, length), jnp.bfloat16),
            pltpu.VMEM((2, length, length), jnp.bfloat16),
            pltpu.VMEM((2, length, QB), jnp.float32),
            pltpu.VMEM((2, length, QB), jnp.float32),
        ],
        compiler_params=pltpu.CompilerParams(vmem_limit_bytes=20 << 20),
        name="attend_heads_back",
    )(query, keys, values, grad, table, rows)
LANES = 128
STRIP = 64
EDGE = 32


def mix_kernel(linear_ref, gate_ref, taps_ref, mixed_ref, sums_ref, padded_ref, total_ref):
    length = linear_ref.shape[0]
    padded_ref[0:EDGE] = jnp.zeros((EDGE, LANES), jnp.float32)
    padded_ref[EDGE : EDGE + length] = linear_ref[...] * jax.nn.sigmoid(gate_ref[...])

    def strip(index, carry):
        begin = pl.multiple_of(index * STRIP, STRIP)
        total = jnp.zeros((STRIP, LANES), jnp.float32)
        for tap in range(CONV_K):
            total = total + padded_ref[
                pl.ds(begin + EDGE - CONV_K + 1 + tap, STRIP), :
            ] * taps_ref[tap : tap + 1, :]
        mixed_ref[pl.ds(begin, STRIP), :] = total
        return carry

    lax.fori_loop(0, length // STRIP, strip, 0)
    mixed = mixed_ref[...]

    @pl.when(pl.program_id(0) == 0)
    def _():
        total_ref[...] = jnp.zeros_like(total_ref)

    total_ref[0] += mixed
    total_ref[1] += mixed * mixed

    @pl.when(pl.program_id(0) == pl.num_programs(0) - 1)
    def _():
        ones = jnp.ones((8, LANES), jnp.float32)
        sums_ref[...] = jnp.concatenate(
            [
                lax.dot_general(
                    ones,
                    total_ref[place],
                    (((1,), (1,)), ((), ())),
                    precision=lax.Precision.HIGHEST,
                    preferred_element_type=jnp.float32,
                )
                for place in range(2)
            ],
            axis=0,
        )


def mix_channels(linear, gate, taps):
    length, width = linear.shape
    block = pl.BlockSpec((length, LANES), lambda part: (0, part))
    mixed, sums = pl.pallas_call(
        mix_kernel,
        out_shape=(
            jax.ShapeDtypeStruct((length, width), jnp.float32),
            jax.ShapeDtypeStruct((16, length), jnp.float32),
        ),
        grid=(width // LANES,),
        in_specs=[block, block, pl.BlockSpec((EDGE, LANES), lambda part: (0, part))],
        out_specs=(block, pl.BlockSpec((16, length), lambda part: (0, 0))),
        scratch_shapes=[
            pltpu.VMEM((EDGE + length, LANES), jnp.float32),
            pltpu.VMEM((2, length, LANES), jnp.float32),
        ],
        compiler_params=pltpu.CompilerParams(vmem_limit_bytes=8 << 20),
        name="mix_channels",
    )(linear, gate, taps)
    return mixed, jnp.concatenate([sums[0:1], sums[8:9]], axis=0)


def mix_back_kernel(
    grad_ref,
    linear_ref,
    gate_ref,
    taps_ref,
    linear_grad_ref,
    gating_grad_ref,
    taps_grad_ref,
    padded_ref,
    tail_ref,
    total_ref,
):
    length = linear_ref.shape[0]
    padded_ref[0:EDGE] = jnp.zeros((EDGE, LANES), jnp.float32)
    padded_ref[EDGE : EDGE + length] = linear_ref[...] * jax.nn.sigmoid(gate_ref[...])
    tail_ref[0:length] = grad_ref[...]
    tail_ref[length : length + EDGE] = jnp.zeros((EDGE, LANES), jnp.float32)
    total_ref[...] = jnp.zeros_like(total_ref)

    def strip(index, carry):
        begin = pl.multiple_of(index * STRIP, STRIP)
        here = pl.ds(begin, STRIP)
        grad = tail_ref[here, :]
        total = jnp.zeros((STRIP, LANES), jnp.float32)
        for tap in range(CONV_K):
            total = total + tail_ref[
                pl.ds(begin + CONV_K - 1 - tap, STRIP), :
            ] * taps_ref[tap : tap + 1, :]
            weighed = grad * padded_ref[pl.ds(begin + EDGE - CONV_K + 1 + tap, STRIP), :]
            total_ref[tap] += jnp.sum(weighed.reshape(STRIP // 8, 8, LANES), axis=0)
        sigma = jax.nn.sigmoid(gate_ref[here, :])
        low = total * sigma
        linear_grad_ref[here, :] = narrow(low)
        gating_grad_ref[here, :] = narrow(low * linear_ref[here, :] * (1.0 - sigma))
        return carry

    lax.fori_loop(0, length // STRIP, strip, 0)
    for tap in range(CONV_K):
        taps_grad_ref[tap : tap + 1, :] = jnp.sum(total_ref[tap], axis=0, keepdims=True)
    taps_grad_ref[CONV_K:EDGE, :] = jnp.zeros((EDGE - CONV_K, LANES), jnp.float32)


def mix_channels_back(grad, linear, gate, taps):
    length, width = linear.shape
    block = pl.BlockSpec((length, LANES), lambda part: (0, part))
    edge = pl.BlockSpec((EDGE, LANES), lambda part: (0, part))
    return pl.pallas_call(
        mix_back_kernel,
        out_shape=(
            jax.ShapeDtypeStruct((length, width), jnp.bfloat16),
            jax.ShapeDtypeStruct((length, width), jnp.bfloat16),
            jax.ShapeDtypeStruct((EDGE, width), jnp.float32),
        ),
        grid=(width // LANES,),
        in_specs=[block, block, block, edge],
        out_specs=(block, block, edge),
        scratch_shapes=[
            pltpu.VMEM((EDGE + length, LANES), jnp.float32),
            pltpu.VMEM((EDGE + length, LANES), jnp.float32),
            pltpu.VMEM((EDGE, 8, LANES), jnp.float32),
        ],
        compiler_params=pltpu.CompilerParams(vmem_limit_bytes=8 << 20),
        name="mix_channels_back",
    )(grad, linear, gate, taps)


def feed_forward(rows, gain, shift, up_weight, up_bias, down_weight):
    normed, center, inverse = layer_norm(rows, gain, shift)
    normed = narrow(normed)
    before = product(normed, up_weight) + up_bias
    hidden = narrow(before * jax.nn.sigmoid(before))
    return product(hidden, down_weight), (rows, center, inverse, normed, before, hidden)


def feed_back(incoming, kept, up_weight, down_weight):
    before = kept[4]
    branch_grad = 0.5 * incoming
    spread = narrow(branch_grad)
    sigma = jax.nn.sigmoid(before)
    before_grad = product_right(spread, down_weight) * sigma * (1.0 + before * (1.0 - sigma))
    before_low = narrow(before_grad)
    share = product_right(before_low, up_weight)
    return share, spread, before_low, jnp.sum(before_grad, axis=0), jnp.sum(branch_grad, axis=0)


def residual_back(incoming, normed_grad, kept, gain):
    rows, center, inverse = kept[:3]
    normal = (rows - center) * inverse
    result, gain_grad, shift_grad = norm_back(normed_grad, normal, inverse, gain)
    return incoming + result, gain_grad, shift_grad


def attend(
    rows, gain, shift, query_weight, query_bias, key_weight, value_weight, value_bias, output_weight, table
):
    normed, center, inverse = layer_norm(rows, gain, shift)
    normed = narrow(normed)
    query = narrow(product(normed, query_weight) + query_bias)
    keys = narrow(product(normed, key_weight))
    values = narrow(product(normed, value_weight) + value_bias)
    context = attend_heads(query, keys, values, table)
    return (
        product(context, output_weight),
        (rows, center, inverse, normed, query, keys, values, context),
    )


def attend_back(
    incoming, kept, query_weight, key_weight, value_weight, output_weight, table, table_rows
):
    query, keys, values = kept[4:7]
    spread = narrow(incoming)
    context_grad = narrow(product_right(spread, output_weight))
    query_low, key_low, value_low, query_sum, value_sum, table_grad = attend_heads_back(
        query, keys, values, context_grad, table, table_rows
    )
    query_low, key_low, value_low = yield Met([query_low, key_low, value_low])
    share = (
        product_right(query_low, query_weight)
        + product_right(key_low, key_weight)
        + product_right(value_low, value_weight)
    )
    return (
        share,
        spread,
        (query_low, key_low, value_low),
        query_sum[0],
        value_sum[0],
        jnp.sum(incoming, axis=0),
        table_grad,
    )


def mix(rows, gain, shift, pointwise_in, taps):
    normed, center, inverse = layer_norm(rows, gain, shift)
    normed = narrow(normed)
    linear = product(normed, pointwise_in[0])
    gate = product(normed, pointwise_in[1])
    mixed, sums = yield Met(mix_channels(linear, gate, taps))
    return mixed, wide_sum(sums), (rows, center, inverse, normed, linear, gate)


def convolve(mixed, sums, depth_gain, depth_shift, pointwise_out):
    center = (sums[0] / D)[:, None]
    channel_inverse = lax.rsqrt(sums[1][:, None] / D - center * center + epsilon)
    channel_normal = (mixed - center) * channel_inverse
    shaped = channel_normal * depth_gain + depth_shift
    active = narrow(shaped * jax.nn.sigmoid(shaped))
    return product(active, pointwise_out), (channel_inverse, channel_normal, shaped, active)


def shape_back(incoming, shape_kept, depth_gain, pointwise_out):
    channel_inverse, channel_normal, shaped, active = shape_kept
    spread = narrow(incoming)
    sigma = jax.nn.sigmoid(shaped)
    shaped_grad = product_right(spread, pointwise_out) * sigma * (1.0 + shaped * (1.0 - sigma))
    scaled = shaped_grad * depth_gain
    sums = wide_sum(
        jnp.stack([jnp.sum(scaled, axis=-1), jnp.sum(scaled * channel_normal, axis=-1)])
    )
    return (
        spread,
        scaled,
        sums,
        jnp.sum(shaped_grad * channel_normal, axis=0),
        jnp.sum(shaped_grad, axis=0),
    )


def convolve_back(scaled, sums, kept, shape_kept, pointwise_in, taps):
    linear, gate = kept[4:6]
    channel_inverse, channel_normal = shape_kept[:2]
    mixed_grad = channel_inverse * (
        scaled - (sums[0] / D)[:, None] - channel_normal * (sums[1] / D)[:, None]
    )
    linear_low, gating_low, taps_grad = mix_channels_back(mixed_grad, linear, gate, taps)
    share = product_right(linear_low, pointwise_in[0]) + product_right(gating_low, pointwise_in[1])
    return share, linear_low, gating_low, taps_grad[:CONV_K]


def total(parts):
    result = parts[0]
    for part in parts[1:]:
        result = result + part
    return result


def weight_grad_kernel(count, *refs):
    total = product_left(refs[0][...], refs[1][...])
    for place in range(1, count):
        total = total + product_left(refs[2 * place][...], refs[2 * place + 1][...])
    refs[2 * count][...] = narrow(total)


def tile_of(size, limit):
    tile = size
    while tile > limit:
        tile //= 2
    return tile


def weight_grad(lefts, rights):
    length, rows = lefts[0].shape
    columns = rights[0].shape[1]
    row_tile, column_tile = tile_of(rows, 1024), tile_of(columns, 1024)
    operands = [value for pair in zip(lefts, rights) for value in pair]
    return pl.pallas_call(
        functools.partial(weight_grad_kernel, len(lefts)),
        out_shape=jax.ShapeDtypeStruct((rows, columns), jnp.bfloat16),
        grid=(rows // row_tile, columns // column_tile),
        in_specs=[
            pl.BlockSpec((length, row_tile), lambda row, column: (0, row)),
            pl.BlockSpec((length, column_tile), lambda row, column: (0, column)),
        ]
        * len(lefts),
        out_specs=pl.BlockSpec((row_tile, column_tile), lambda row, column: (row, column)),
        compiler_params=pltpu.CompilerParams(vmem_limit_bytes=24 << 20),
        name="weight_grad",
    )(*operands)


class Gradients:
    def __init__(self, flow, count):
        self.flow = flow
        self.count = count
        self.parts = {}
        self.jobs = {}

    def add(self, name, part):
        parts = self.parts.setdefault(name, [])
        parts.append(part)
        return len(parts) == self.count

    def maker(self, name):
        parts = self.parts[name]
        return lambda: [
            weight_grad([part[place][0] for part in parts], [part[place][1] for part in parts])
            for place in range(len(parts[0]))
        ]

    def weights(self, name, pairs, width, delay=0, eager=False):
        if self.add(name, pairs):
            self.jobs[name] = self.flow.launch(scatter_job(self.maker(name), delay, width, eager))

    def sums(self, name, values):
        self.add(name, values)

    def reduce_sums(self, name, groups):
        values = []
        for group in groups:
            parts = self.parts[group]
            values.extend(total([part[place] for part in parts]) for place in range(len(parts[0])))
        self.jobs[name] = self.flow.launch(small_job(values))

    def whole(self, name, pairs):
        if self.add(name, pairs):
            self.jobs[name] = self.flow.launch(sum_job(self.maker(name)))

    def gather(self, name, members, turns=None):
        if members[-1] in self.jobs and name not in self.jobs:
            self.jobs[name] = self.flow.launch(
                gather_job([self.jobs[member] for member in members], turns)
            )

    def result(self, name):
        return self.jobs[name].result


def per_device(
    tokens,
    clip_count,
    first_norm_gain,
    first_norm_shift,
    first_up_weight,
    first_up_bias,
    first_down_weight,
    first_down_bias,
    attend_norm_gain,
    attend_norm_shift,
    query_weight,
    query_bias,
    key_weight,
    value_weight,
    value_bias,
    output_weight,
    output_bias,
    relative_table,
    convolve_norm_gain,
    convolve_norm_shift,
    pointwise_in,
    depthwise_weight,
    depth_norm_gain,
    depth_norm_shift,
    pointwise_out,
    second_norm_gain,
    second_norm_shift,
    second_up_weight,
    second_up_bias,
    second_down_weight,
    second_down_bias,
    final_norm_gain,
    final_norm_shift,
    cotangent,
):
    slots = range(tokens.shape[0])
    live_count = clip_count[0]
    first_gain = widen(first_norm_gain)
    attend_gain = widen(attend_norm_gain)
    convolve_gain = widen(convolve_norm_gain)
    second_gain = widen(second_norm_gain)
    final_gain = widen(final_norm_gain)
    taps = jnp.pad(widen(depthwise_weight), ((0, EDGE - CONV_K), (0, 0)))
    depth_gain = widen(depth_norm_gain)
    table, table_rows = table_forms(relative_table)
    flow = Flow()
    grads = Gradients(flow, len(slots))
    outputs = {}
    input_grads = {}
    count_job = flow.launch(small_job([jnp.full((1, 128), widen(live_count), jnp.float32)]))

    def clip(slot):
        live = (live_count > slot).astype(jnp.float32)
        rows = widen((yield Gathered(tokens[slot])))
        share, first_kept = feed_forward(
            rows,
            first_gain,
            widen(first_norm_shift),
            first_up_weight,
            widen(first_up_bias),
            first_down_weight,
        )
        rows = rows + 0.5 * ((yield Summed(share)) + widen(first_down_bias))
        share, attend_kept = attend(
            rows,
            attend_gain,
            widen(attend_norm_shift),
            query_weight,
            widen(query_bias),
            key_weight,
            value_weight,
            widen(value_bias),
            output_weight,
            table,
        )
        rows = rows + (yield Summed(share)) + widen(output_bias)
        mixed, sums, convolve_kept = yield from mix(
            rows, convolve_gain, widen(convolve_norm_shift), pointwise_in, taps
        )
        share, shape_kept = convolve(
            mixed, sums, depth_gain, widen(depth_norm_shift), pointwise_out
        )
        rows = rows + (yield Summed(share))
        share, second_kept = feed_forward(
            rows,
            second_gain,
            widen(second_norm_shift),
            second_up_weight,
            widen(second_up_bias),
            second_down_weight,
        )
        last = own_rows(rows) + 0.5 * ((yield Scattered(share)) + widen(second_down_bias))
        normed, center, inverse = layer_norm(last, final_gain, widen(final_norm_shift))
        outputs[slot] = narrow(normed * live)
        grad, gain_grad, shift_grad = norm_back(
            widen(cotangent[slot]) * live, (last - center) * inverse, inverse, final_gain
        )
        grads.sums("final", [gain_grad, shift_grad])

        grad = widen((yield Gathered(narrow(grad))))
        share, spread, before_low, up_sum, down_sum = feed_back(
            grad, second_kept, second_up_weight, second_down_weight
        )
        grads.whole("second_both", [(second_kept[5], spread), (second_kept[3], before_low)])
        normed_grad = yield Summed(share)
        grad, gain_grad, shift_grad = residual_back(grad, normed_grad, second_kept, second_gain)
        grads.sums("second", [up_sum, down_sum, gain_grad, shift_grad])

        spread, scaled, sums, depth_gain_sum, depth_shift_sum = shape_back(
            grad, shape_kept, depth_gain, pointwise_out
        )
        share, linear_low, gating_low, depthwise_sum = convolve_back(
            scaled, sums, convolve_kept, shape_kept, pointwise_in, taps
        )
        grads.weights(
            "convolve",
            [
                (convolve_kept[3], linear_low),
                (convolve_kept[3], gating_low),
                (shape_kept[3], spread),
            ],
            linear_low.shape[1],
        )
        normed_grad = yield Summed(share)
        grad, gain_grad, shift_grad = residual_back(
            grad, normed_grad, convolve_kept, convolve_gain
        )
        grads.sums(
            "convolve_sums", [depth_gain_sum, depth_shift_sum, depthwise_sum, gain_grad, shift_grad]
        )

        share, spread, lows, query_sum, value_sum, output_sum, table_sum = yield from attend_back(
            grad,
            attend_kept,
            query_weight,
            key_weight,
            value_weight,
            output_weight,
            table,
            table_rows,
        )
        grads.weights(
            "attend",
            [(attend_kept[7], spread)] + [(attend_kept[3], low) for low in lows],
            lows[0].shape[1],
        )
        grads.sums("attend_sums", [query_sum, value_sum, output_sum, table_sum])
        grads.gather("middle", ["convolve", "attend"])
        normed_grad = yield Summed(share)
        grad, gain_grad, shift_grad = residual_back(grad, normed_grad, attend_kept, attend_gain)
        grads.sums("attend_norm", [gain_grad, shift_grad])

        share, spread, before_low, up_sum, down_sum = feed_back(
            grad, first_kept, first_up_weight, first_down_weight
        )
        grads.weights("first_down", [(first_kept[5], spread)], spread.shape[1], eager=True)
        grads.weights("first_up", [(first_kept[3], before_low)], spread.shape[1], 0, eager=True)
        grads.gather("first_both", ["first_down", "first_up"])
        normed_grad = yield Scattered(share)
        input_grads[slot], gain_grad, shift_grad = residual_back(
            own_rows(grad),
            normed_grad,
            [own_rows(kept) for kept in first_kept[:3]],
            first_gain,
        )
        grads.sums("first", [up_sum, down_sum])
        grads.sums("first_norm", [gain_grad, shift_grad])

    flow.run([clip(slot) for slot in slots])
    own = [
        total([part[place] for part in grads.parts[group]])
        for group, place in (
            ("final", 0),
            ("final", 1),
            ("first_norm", 0),
            ("first_norm", 1),
            ("attend_sums", 3),
        )
    ]
    flat = wide_sum(jnp.concatenate([value.reshape(-1) for value in own]))
    shared = []
    for value in own:
        shared.append(flat[: value.size].reshape(value.shape))
        flat = flat[value.size :]
    grads.parts["final"] = [shared[:2]]
    grads.parts["first_norm"] = [shared[2:4]]
    grads.parts["attend_sums"] = [
        [total([part[place] for part in grads.parts["attend_sums"]]) for place in range(3)]
        + shared[4:]
    ]
    grads.reduce_sums(
        "sums",
        [
            "final",
            "second",
            "convolve_sums",
            "attend_sums",
            "attend_norm",
            "first",
            "first_norm",
        ],
    )
    flow.drain()

    clips = count_job.result[0][0, 0]
    early, late = grads.result("sums")[:15], grads.result("sums")[15:]
    second_down, second_up = grads.result("second_both")
    linear, gating, point_out, output_grad, query_grad, key_grad, value_grad = grads.result("middle")
    first_down, first_up = grads.result("first_both")
    table_grad = early[14].T[: relative_table.shape[0]]
    every = (
        late[4],
        late[5],
        first_up,
        late[2],
        first_down,
        late[3],
        late[0],
        late[1],
        query_grad,
        early[11],
        key_grad,
        value_grad,
        early[12],
        output_grad,
        early[13],
        table_grad,
        early[9],
        early[10],
        jnp.stack([linear, gating]),
        early[8],
        early[6],
        early[7],
        point_out,
        early[4],
        early[5],
        second_up,
        early[2],
        second_down,
        early[3],
        early[0],
        early[1],
    )
    return (
        jnp.stack([outputs[slot] for slot in slots]),
        jnp.stack([input_grads[slot] for slot in slots]),
    ) + tuple(widen(value) / clips for value in every)


def solution(mesh):
    placed = (
        P("dp", "tensor", None),
        P("dp"),
        P(),
        P(),
        P(None, "tensor"),
        P("tensor"),
        P("tensor", None),
        P(),
        P(),
        P(),
        P(None, "tensor"),
        P("tensor"),
        P(None, "tensor"),
        P(None, "tensor"),
        P("tensor"),
        P("tensor", None),
        P(),
        P(),
        P(),
        P(),
        P(None, None, "tensor"),
        P(None, "tensor"),
        P("tensor"),
        P("tensor"),
        P("tensor", None),
        P(),
        P(),
        P(None, "tensor"),
        P("tensor"),
        P("tensor", None),
        P(),
        P(),
        P(),
        P("dp", "tensor", None),
    )
    return jax.shard_map(
        per_device,
        mesh=mesh,
        in_specs=placed,
        out_specs=(
            P("dp", "tensor", None),
            P("dp", "tensor", None),
            P(),
            P(),
            P(None, "tensor"),
            P("tensor"),
            P("tensor", None),
            P(),
            P(),
            P(),
            P(None, "tensor"),
            P("tensor"),
            P(None, "tensor"),
            P(None, "tensor"),
            P("tensor"),
            P("tensor", None),
            P(),
            P(),
            P(),
            P(),
            P(None, None, "tensor"),
            P(None, "tensor"),
            P("tensor"),
            P("tensor"),
            P("tensor", None),
            P(),
            P(),
            P(None, "tensor"),
            P("tensor"),
            P("tensor", None),
            P(),
            P(),
            P(),
        ),
        check_vma=False,
    )
```

```python
import functools
import math

import jax
import jax.numpy as jnp
from jax import lax
from jax.experimental import pallas as pl
from jax.experimental.pallas import tpu as pltpu
from jax.sharding import PartitionSpec as P

D = 1024
HEAD_DIM = 64
CONV_K = 31
BACK = 64
AHEAD = 8

epsilon = 1e-05


def product(left, right):
    return jnp.dot(left, right, preferred_element_type=jnp.float32)


def product_left(left, right):
    return lax.dot_general(
        left, right, (((0,), (0,)), ((), ())), preferred_element_type=jnp.float32
    )


def product_right(left, right):
    return lax.dot_general(
        left, right, (((1,), (1,)), ((), ())), preferred_element_type=jnp.float32
    )


def widen(value):
    return value.astype(jnp.float32)


def narrow(value):
    return value.astype(jnp.bfloat16)


def norm_stats(values):
    center = jnp.mean(values, axis=-1, keepdims=True)
    offset = values - center
    inverse = lax.rsqrt(jnp.mean(offset * offset, axis=-1, keepdims=True) + epsilon)
    return center, inverse


def layer_norm(values, gain, shift):
    center, inverse = norm_stats(values)
    normal = (values - center) * inverse
    return normal * gain + shift, center, inverse


def norm_back(incoming, normal, inverse, gain):
    scaled = incoming * gain
    first_mean = jnp.mean(scaled, axis=-1, keepdims=True)
    second_mean = jnp.mean(scaled * normal, axis=-1, keepdims=True)
    result = inverse * (scaled - first_mean - normal * second_mean)
    return (result, jnp.sum(incoming * normal, axis=0), jnp.sum(incoming, axis=0))


def paired():
    return lax.axis_size("tensor") == 2


def swap(values):
    return lax.ppermute(values, "tensor", [(0, 1), (1, 0)])


def rows_of(values, which):
    count = values.shape[0] // lax.axis_size("tensor")
    return lax.dynamic_slice_in_dim(values, which * count, count, 0)


def own_rows(values):
    return rows_of(values, lax.axis_index("tensor"))


def wide_sum(share):
    if paired():
        count = 2 * lax.axis_size("dp")
        pairs = [(place, place ^ 1) for place in reversed(range(count))]
        return share + lax.ppermute(share, ("dp", "tensor"), pairs)
    return lax.psum(share, "tensor")


class Gathered:
    def __init__(self, values):
        self.sent = values

    def move(self, sent):
        if paired():
            return swap(sent)
        return lax.all_gather(sent, "tensor", axis=0, tiled=True)

    def finish(self, sent, got):
        if not paired():
            return got
        first = lax.axis_index("tensor") == 0
        return jnp.concatenate(
            [jnp.where(first, sent, got), jnp.where(first, got, sent)], axis=0
        )


class Summed:
    def __init__(self, share):
        self.sent = narrow(share)

    def move(self, sent):
        if paired():
            return swap(sent)
        return lax.psum(sent, "tensor")

    def finish(self, sent, got):
        if not paired():
            return widen(got)
        return widen(sent) + widen(got)


class Scattered:
    def __init__(self, share):
        self.own = None
        if paired():
            self.own = own_rows(share)
            self.sent = narrow(rows_of(share, 1 - lax.axis_index("tensor")))
        else:
            self.sent = narrow(share)

    def move(self, sent):
        if paired():
            return swap(sent)
        return lax.psum_scatter(sent, "tensor", scatter_dimension=0, tiled=True)

    def finish(self, sent, got):
        if self.own is None:
            return widen(got)
        return self.own + widen(got)


class Met:
    def __init__(self, values):
        self.values = list(values)


class Job:
    def __init__(self, steps):
        self.steps = steps
        self.result = None
        self.waiting = []
        self.active = True
        self.advance(None)

    def advance(self, values):
        try:
            self.waiting = list(self.steps.send(values))
        except StopIteration as ended:
            self.active = False
            self.waiting = []
            self.result = ended.value


class Flow:
    def __init__(self):
        self.jobs = []

    def launch(self, steps):
        job = Job(steps)
        self.jobs.append(job)
        return job

    def turn(self, held, jobs=True):
        active = [job for job in self.jobs if jobs and job.active]
        flat = list(held)
        for job in active:
            flat.extend(job.waiting)
        if len(flat) > 1:
            flat = list(lax.optimization_barrier(tuple(flat)))
        begin = len(held)
        moved = []
        for job in active:
            moved.append(flat[begin : begin + len(job.waiting)])
            begin += len(job.waiting)
        return flat[: len(held)], list(zip(active, moved))

    def run(self, clips):
        under_way = None
        arrived = {}

        def settle(held, jobs=True):
            extra = [] if under_way is None else [under_way[1].sent, under_way[2]]
            if under_way is not None:
                arrived[under_way[0]] = (under_way[1], *extra)
            waiting = list(arrived)
            extra = [value for place in waiting for value in arrived[place][1:]]
            out, moved = self.turn(held + extra, jobs)
            for index, place in enumerate(waiting):
                begin = len(held) + 2 * index
                arrived[place] = (arrived[place][0], *out[begin : begin + 2])
            for job, values in moved:
                job.advance(values)
            return out[: len(held)]

        queue = list(range(len(clips)))
        started = set()
        while queue:
            place = queue.pop(0)
            if under_way is not None and under_way[0] == place:
                settle([])
                under_way = None
            try:
                if place in started:
                    earlier, sent, got = arrived.pop(place)
                    request = clips[place].send(earlier.finish(sent, got))
                else:
                    started.add(place)
                    request = next(clips[place])
                while isinstance(request, Met):
                    values = settle(request.values, False)
                    under_way = None
                    request = clips[place].send(values)
            except StopIteration:
                continue
            (sent,) = settle([request.sent])
            request.sent = sent
            under_way = (place, request, request.move(sent))
            queue.append(place)

    def drain(self):
        while any(job.active for job in self.jobs):
            _, moved = self.turn([])
            for job, values in moved:
                job.advance(values)


def dp_grid():
    return lax.axis_size("dp") == 16


def dp_bit(bit):
    return (lax.axis_index("dp") // bit) % 2


def dp_swap(values, bit):
    return lax.ppermute(values, "dp", [(place, place ^ bit) for place in range(16)])


def piece_of(values, which, axis):
    return lax.dynamic_index_in_dim(values, which, axis, keepdims=False)


def add_low(left, right):
    return narrow(widen(left) + widen(right))


def unstack_columns(shards, values):
    width = shards.shape[-1]
    results = []
    begin = 0
    for value in values:
        size = value.shape[0] // shards.shape[0]
        pieces = []
        for _ in range(0, value.shape[1], width):
            pieces.append(shards[:, begin : begin + size].reshape(value.shape[0], width))
            begin += size
        results.append(jnp.concatenate(pieces, axis=1) if len(pieces) > 1 else pieces[0])
    return results


def split_rows(value):
    return value.reshape(2, 2, 2, 2, value.shape[0] // 16, value.shape[1])


def scatter_job(make, delay, width, eager):
    if not eager:
        yield []
    values = [narrow(value) for value in make()]
    if not dp_grid():
        return values, [lax.psum(value, "dp") for value in values]
    parts = []
    for value in values:
        for start in range(0, value.shape[1], width):
            parts.append(split_rows(value[:, start : start + width]))
    core, side, near, far = [dp_bit(bit) for bit in (1, 2, 4, 8)]
    sent = jnp.concatenate([piece_of(part, 1 - core, 3) for part in parts], axis=3)
    kept = jnp.concatenate([piece_of(part, core, 3) for part in parts], axis=3)
    part = add_low(kept, dp_swap(sent, 1))
    sent, kept = yield [piece_of(part, 1 - side, 2), piece_of(part, side, 2)]
    for _ in range(delay):
        yield []
    part = add_low(kept, dp_swap(sent, 2))
    sent, kept = yield [piece_of(part, 1 - near, 1), piece_of(part, near, 1)]
    part = add_low(kept, dp_swap(sent, 4))
    shard = add_low(piece_of(part, far, 0), dp_swap(piece_of(part, 1 - far, 0), 8))
    (shard,) = yield [shard]
    return values, shard


def sum_job(make):
    values = yield [narrow(value) for value in make()]
    summed = [lax.psum(value, "dp") for value in values]
    for _ in range(5):
        yield []
    return (yield summed)


def gather_job(jobs, turns):
    while any(job.active for job in jobs):
        yield []
    values = [value for job in jobs for value in job.result[0]]
    if not dp_grid():
        return [value for job in jobs for value in job.result[1]]
    shards = jnp.concatenate([job.result[1] for job in jobs], axis=0)
    whole = lax.all_gather(shards, "dp", axis=0)
    if turns is not None:
        for _ in range(turns):
            yield []
        (whole,) = yield [whole]
    return unstack_columns(whole, values)


def small_job(values):
    flat = jnp.concatenate([value.reshape(-1) for value in values])
    if dp_grid():
        for bit in (1, 2, 4, 8):
            (got,) = yield [dp_swap(flat, bit)]
            flat = flat + got
    else:
        flat = lax.psum(flat, "dp")
    results = []
    start = 0
    for value in values:
        results.append(flat[start : start + value.size].reshape(value.shape))
        start += value.size
    return results


SCALE = 1.0 / math.sqrt(HEAD_DIM)
PAIR = 2 * HEAD_DIM
QB = 128
WINDOW = 3 * QB
ROWS = 32


def keep_head(block, head):
    inside = lax.broadcasted_iota(jnp.int32, block.shape, 1) < HEAD_DIM
    if head == 1:
        inside = jnp.logical_not(inside)
    return jnp.where(inside, block, jnp.zeros_like(block))


def strip_place(begin, length):
    return (
        lax.broadcasted_iota(jnp.int32, (ROWS, length), 1)
        - lax.broadcasted_iota(jnp.int32, (ROWS, length), 0)
        - begin
    )


def strip_probs(content, relative, begin, place):
    length = content.shape[1]
    block = begin // QB
    low = max(block - 1, 0) * QB
    high = min(block + 2, length // QB) * QB
    before = relative[:, 0:1]
    after = relative[:, BACK + AHEAD : BACK + AHEAD + 1]
    turned = pltpu.roll(relative, (begin + QB - BACK) % QB, 1, stride=1, stride_axis=0)
    parts = []
    for start in range(0, length, QB):
        if start < low:
            parts.append(jnp.broadcast_to(before, (ROWS, QB)))
        elif start >= high:
            parts.append(jnp.broadcast_to(after, (ROWS, QB)))
        else:
            here = place[:, start : start + QB]
            parts.append(
                jnp.where(here < -BACK, before, jnp.where(here > AHEAD, after, turned))
            )
    scores = (content + jnp.concatenate(parts, axis=1)) * SCALE
    weights = jnp.exp(scores - jnp.max(scores, axis=-1, keepdims=True))
    return weights * (1.0 / jnp.sum(weights, axis=-1, keepdims=True))


def attend_kernel(query_ref, key_ref, value_ref, table_ref, context_ref, score_ref, probs_ref, band_ref):
    length = query_ref.shape[0]
    parts = []
    for head in range(2):
        query = keep_head(query_ref[...], head)
        score_ref[head] = product_right(query, key_ref[...])
        band_ref[head] = product(query, table_ref[...])
        for begin in range(0, length, ROWS):
            rows = slice(begin, begin + ROWS)
            probs_ref[head, rows] = narrow(
                strip_probs(
                    score_ref[head, rows],
                    band_ref[head, rows],
                    begin,
                    strip_place(begin, length),
                )
            )
        parts.append(product(probs_ref[head], value_ref[...]))
    lane = lax.broadcasted_iota(jnp.int32, parts[0].shape, 1)
    context_ref[...] = narrow(jnp.where(lane < HEAD_DIM, parts[0], parts[1]))


def gather_block(low_block, block, blocks, flip):
    low = max(block - 1, 0)
    high = min(block + 2, blocks)
    parts = []
    if block == 0:
        parts.append(jnp.zeros((QB, QB), jnp.bfloat16))
    parts.append(low_block[:, low * QB : high * QB])
    if block == blocks - 1:
        parts.append(jnp.zeros((QB, QB), jnp.bfloat16))
    reversed_rows = product(flip, jnp.concatenate(parts, axis=1))
    moved = pltpu.roll(
        reversed_rows, WINDOW - (QB - BACK) - (QB - 1), 1, stride=1, stride_axis=0
    )[:, :QB]
    return product(flip, narrow(moved))


def attend_back_kernel(
    query_ref,
    key_ref,
    value_ref,
    grad_ref,
    table_ref,
    rows_ref,
    query_grad_ref,
    key_grad_ref,
    value_grad_ref,
    query_sum_ref,
    value_sum_ref,
    table_grad_ref,
    score_ref,
    wide_ref,
    probs_ref,
    low_ref,
    band_ref,
    ends_ref,
):
    @pl.when(pl.program_id(0) == 0)
    def _():
        table_grad_ref[...] = jnp.zeros_like(table_grad_ref)

    length = query_ref.shape[0]
    blocks = length // QB
    query_turned = narrow(widen(query_ref[...]).T)
    grad_turned = narrow(widen(grad_ref[...]).T)
    flip = narrow(
        (
            lax.broadcasted_iota(jnp.int32, (QB, QB), 0)
            + lax.broadcasted_iota(jnp.int32, (QB, QB), 1)
            == QB - 1
        ).astype(jnp.float32)
    )
    lane = lax.broadcasted_iota(jnp.int32, (ROWS, QB), 1)
    query_parts = []
    key_parts = []
    value_parts = []
    for head in range(2):
        piece = slice(head * HEAD_DIM, (head + 1) * HEAD_DIM)
        query = keep_head(query_ref[...], head)
        score_ref[head] = product_right(query, key_ref[...])
        band_ref[head] = product(query, table_ref[...])
        wide_ref[head] = product_right(keep_head(grad_ref[...], head), value_ref[...])
        for begin in range(0, length, ROWS):
            rows = slice(begin, begin + ROWS)
            place = strip_place(begin, length)
            probs = strip_probs(score_ref[head, rows], band_ref[head, rows], begin, place)
            probs_ref[head, rows] = narrow(probs)
            probs_grad = wide_ref[head, rows]
            delta = jnp.sum(probs * probs_grad, axis=-1, keepdims=True)
            score_grad = narrow(probs * (probs_grad - delta))
            low_ref[head, rows] = score_grad
            wide = widen(score_grad)
            back = jnp.sum(jnp.where(place <= -BACK, wide, 0.0), axis=-1, keepdims=True)
            ahead = jnp.sum(jnp.where(place >= AHEAD, wide, 0.0), axis=-1, keepdims=True)
            ends_ref[head, rows] = jnp.where(
                lane == 0, back, jnp.where(lane == BACK + AHEAD, ahead, 0.0)
            )
        for block in range(blocks):
            rows = slice(block * QB, (block + 1) * QB)
            inner = gather_block(low_ref[head, rows], block, blocks, flip)
            column = lax.broadcasted_iota(jnp.int32, (QB, QB), 1)
            inside = jnp.logical_and(column > 0, column < BACK + AHEAD)
            band_ref[head, rows] = jnp.where(inside, inner, ends_ref[head, rows])
        value_parts.append(product(grad_turned[piece], probs_ref[head]))
        key_parts.append(product(query_turned[piece], low_ref[head]))
        band = band_ref[head]
        band_high = narrow(band)
        band_low = narrow(band - widen(band_high))
        query_parts.append(
            product(low_ref[head], key_ref[...])
            + product(band_high, rows_ref[...])
            + product(band_low, rows_ref[...])
        )
        table_grad_ref[...] += SCALE * (
            product(query_turned[piece], band_high) + product(query_turned[piece], band_low)
        )
    lane = lax.broadcasted_iota(jnp.int32, query_parts[0].shape, 1)
    query_grad = SCALE * jnp.where(lane < HEAD_DIM, query_parts[0], query_parts[1])
    query_grad_ref[...] = narrow(query_grad)
    query_sum_ref[...] = jnp.sum(query_grad, axis=0, keepdims=True)
    key_grad_ref[...] = narrow(SCALE * jnp.concatenate(key_parts, axis=0).T)
    value_grad = jnp.concatenate(value_parts, axis=0).T
    value_grad_ref[...] = narrow(value_grad)
    value_sum_ref[...] = jnp.sum(value_grad, axis=0, keepdims=True)


def pair_spec(length):
    return pl.BlockSpec((length, PAIR), lambda pair: (0, pair))


def fixed_spec(shape):
    return pl.BlockSpec(shape, lambda pair: tuple(0 for _ in shape))


def table_forms(relative_table):
    padded = jnp.pad(relative_table, ((0, QB - relative_table.shape[0]), (0, 0)))
    rows = jnp.concatenate([padded, padded], axis=1)
    return rows.T, rows


def attend_heads(query, keys, values, table):
    length, width = query.shape
    return pl.pallas_call(
        attend_kernel,
        out_shape=jax.ShapeDtypeStruct((length, width), jnp.bfloat16),
        grid=(width // PAIR,),
        in_specs=[pair_spec(length)] * 3 + [fixed_spec((PAIR, QB))],
        out_specs=pair_spec(length),
        scratch_shapes=[
            pltpu.VMEM((2, length, length), jnp.float32),
            pltpu.VMEM((2, length, length), jnp.bfloat16),
            pltpu.VMEM((2, length, QB), jnp.float32),
        ],
        compiler_params=pltpu.CompilerParams(vmem_limit_bytes=16 << 20),
        name="attend_heads",
    )(query, keys, values, table)


def attend_heads_back(query, keys, values, grad, table, rows):
    length, width = query.shape
    sums = pl.BlockSpec((1, PAIR), lambda pair: (0, pair))
    return pl.pallas_call(
        attend_back_kernel,
        out_shape=(
            jax.ShapeDtypeStruct((length, width), jnp.bfloat16),
            jax.ShapeDtypeStruct((length, width), jnp.bfloat16),
            jax.ShapeDtypeStruct((length, width), jnp.bfloat16),
            jax.ShapeDtypeStruct((1, width), jnp.float32),
            jax.ShapeDtypeStruct((1, width), jnp.float32),
            jax.ShapeDtypeStruct((HEAD_DIM, QB), jnp.float32),
        ),
        grid=(width // PAIR,),
        in_specs=[pair_spec(length)] * 4 + [fixed_spec((PAIR, QB)), fixed_spec((QB, PAIR))],
        out_specs=(pair_spec(length),) * 3 + (sums, sums, fixed_spec((HEAD_DIM, QB))),
        scratch_shapes=[
            pltpu.VMEM((2, length, length), jnp.float32),
            pltpu.VMEM((2, length, length), jnp.float32),
            pltpu.VMEM((2, length, length), jnp.bfloat16),
            pltpu.VMEM((2, length, length), jnp.bfloat16),
            pltpu.VMEM((2, length, QB), jnp.float32),
            pltpu.VMEM((2, length, QB), jnp.float32),
        ],
        compiler_params=pltpu.CompilerParams(vmem_limit_bytes=20 << 20),
        name="attend_heads_back",
    )(query, keys, values, grad, table, rows)
LANES = 128
STRIP = 64
EDGE = 32


def mix_kernel(linear_ref, gate_ref, taps_ref, mixed_ref, sums_ref, padded_ref, total_ref):
    length = linear_ref.shape[0]
    padded_ref[0:EDGE] = jnp.zeros((EDGE, LANES), jnp.float32)
    padded_ref[EDGE : EDGE + length] = linear_ref[...] * jax.nn.sigmoid(gate_ref[...])

    def strip(index, carry):
        begin = pl.multiple_of(index * STRIP, STRIP)
        total = jnp.zeros((STRIP, LANES), jnp.float32)
        for tap in range(CONV_K):
            total = total + padded_ref[
                pl.ds(begin + EDGE - CONV_K + 1 + tap, STRIP), :
            ] * taps_ref[tap : tap + 1, :]
        mixed_ref[pl.ds(begin, STRIP), :] = total
        return carry

    lax.fori_loop(0, length // STRIP, strip, 0)
    mixed = mixed_ref[...]

    @pl.when(pl.program_id(0) == 0)
    def _():
        total_ref[...] = jnp.zeros_like(total_ref)

    total_ref[0] += mixed
    total_ref[1] += mixed * mixed

    @pl.when(pl.program_id(0) == pl.num_programs(0) - 1)
    def _():
        ones = jnp.ones((8, LANES), jnp.float32)
        sums_ref[...] = jnp.concatenate(
            [
                lax.dot_general(
                    ones,
                    total_ref[place],
                    (((1,), (1,)), ((), ())),
                    precision=lax.Precision.HIGHEST,
                    preferred_element_type=jnp.float32,
                )
                for place in range(2)
            ],
            axis=0,
        )


def mix_channels(linear, gate, taps):
    length, width = linear.shape
    block = pl.BlockSpec((length, LANES), lambda part: (0, part))
    mixed, sums = pl.pallas_call(
        mix_kernel,
        out_shape=(
            jax.ShapeDtypeStruct((length, width), jnp.float32),
            jax.ShapeDtypeStruct((16, length), jnp.float32),
        ),
        grid=(width // LANES,),
        in_specs=[block, block, pl.BlockSpec((EDGE, LANES), lambda part: (0, part))],
        out_specs=(block, pl.BlockSpec((16, length), lambda part: (0, 0))),
        scratch_shapes=[
            pltpu.VMEM((EDGE + length, LANES), jnp.float32),
            pltpu.VMEM((2, length, LANES), jnp.float32),
        ],
        compiler_params=pltpu.CompilerParams(vmem_limit_bytes=8 << 20),
        name="mix_channels",
    )(linear, gate, taps)
    return mixed, jnp.concatenate([sums[0:1], sums[8:9]], axis=0)


def mix_back_kernel(
    grad_ref,
    linear_ref,
    gate_ref,
    taps_ref,
    linear_grad_ref,
    gating_grad_ref,
    taps_grad_ref,
    padded_ref,
    tail_ref,
    total_ref,
):
    length = linear_ref.shape[0]
    padded_ref[0:EDGE] = jnp.zeros((EDGE, LANES), jnp.float32)
    padded_ref[EDGE : EDGE + length] = linear_ref[...] * jax.nn.sigmoid(gate_ref[...])
    tail_ref[0:length] = grad_ref[...]
    tail_ref[length : length + EDGE] = jnp.zeros((EDGE, LANES), jnp.float32)
    total_ref[...] = jnp.zeros_like(total_ref)

    def strip(index, carry):
        begin = pl.multiple_of(index * STRIP, STRIP)
        here = pl.ds(begin, STRIP)
        grad = tail_ref[here, :]
        total = jnp.zeros((STRIP, LANES), jnp.float32)
        for tap in range(CONV_K):
            total = total + tail_ref[
                pl.ds(begin + CONV_K - 1 - tap, STRIP), :
            ] * taps_ref[tap : tap + 1, :]
            weighed = grad * padded_ref[pl.ds(begin + EDGE - CONV_K + 1 + tap, STRIP), :]
            total_ref[tap] += jnp.sum(weighed.reshape(STRIP // 8, 8, LANES), axis=0)
        sigma = jax.nn.sigmoid(gate_ref[here, :])
        low = total * sigma
        linear_grad_ref[here, :] = narrow(low)
        gating_grad_ref[here, :] = narrow(low * linear_ref[here, :] * (1.0 - sigma))
        return carry

    lax.fori_loop(0, length // STRIP, strip, 0)
    for tap in range(CONV_K):
        taps_grad_ref[tap : tap + 1, :] = jnp.sum(total_ref[tap], axis=0, keepdims=True)
    taps_grad_ref[CONV_K:EDGE, :] = jnp.zeros((EDGE - CONV_K, LANES), jnp.float32)


def mix_channels_back(grad, linear, gate, taps):
    length, width = linear.shape
    block = pl.BlockSpec((length, LANES), lambda part: (0, part))
    edge = pl.BlockSpec((EDGE, LANES), lambda part: (0, part))
    return pl.pallas_call(
        mix_back_kernel,
        out_shape=(
            jax.ShapeDtypeStruct((length, width), jnp.bfloat16),
            jax.ShapeDtypeStruct((length, width), jnp.bfloat16),
            jax.ShapeDtypeStruct((EDGE, width), jnp.float32),
        ),
        grid=(width // LANES,),
        in_specs=[block, block, block, edge],
        out_specs=(block, block, edge),
        scratch_shapes=[
            pltpu.VMEM((EDGE + length, LANES), jnp.float32),
            pltpu.VMEM((EDGE + length, LANES), jnp.float32),
            pltpu.VMEM((EDGE, 8, LANES), jnp.float32),
        ],
        compiler_params=pltpu.CompilerParams(vmem_limit_bytes=8 << 20),
        name="mix_channels_back",
    )(grad, linear, gate, taps)


def feed_forward(rows, gain, shift, up_weight, up_bias, down_weight):
    normed, center, inverse = layer_norm(rows, gain, shift)
    normed = narrow(normed)
    before = product(normed, up_weight) + up_bias
    hidden = narrow(before * jax.nn.sigmoid(before))
    return product(hidden, down_weight), (rows, center, inverse, normed, before, hidden)


def feed_back(incoming, kept, up_weight, down_weight):
    before = kept[4]
    branch_grad = 0.5 * incoming
    spread = narrow(branch_grad)
    sigma = jax.nn.sigmoid(before)
    before_grad = product_right(spread, down_weight) * sigma * (1.0 + before * (1.0 - sigma))
    before_low = narrow(before_grad)
    share = product_right(before_low, up_weight)
    return share, spread, before_low, jnp.sum(before_grad, axis=0), jnp.sum(branch_grad, axis=0)


def residual_back(incoming, normed_grad, kept, gain):
    rows, center, inverse = kept[:3]
    normal = (rows - center) * inverse
    result, gain_grad, shift_grad = norm_back(normed_grad, normal, inverse, gain)
    return incoming + result, gain_grad, shift_grad


def attend(
    rows, gain, shift, query_weight, query_bias, key_weight, value_weight, value_bias, output_weight, table
):
    normed, center, inverse = layer_norm(rows, gain, shift)
    normed = narrow(normed)
    query = narrow(product(normed, query_weight) + query_bias)
    keys = narrow(product(normed, key_weight))
    values = narrow(product(normed, value_weight) + value_bias)
    context = attend_heads(query, keys, values, table)
    return (
        product(context, output_weight),
        (rows, center, inverse, normed, query, keys, values, context),
    )


def attend_back(
    incoming, kept, query_weight, key_weight, value_weight, output_weight, table, table_rows
):
    query, keys, values = kept[4:7]
    spread = narrow(incoming)
    context_grad = narrow(product_right(spread, output_weight))
    query_low, key_low, value_low, query_sum, value_sum, table_grad = attend_heads_back(
        query, keys, values, context_grad, table, table_rows
    )
    query_low, key_low, value_low = yield Met([query_low, key_low, value_low])
    share = (
        product_right(query_low, query_weight)
        + product_right(key_low, key_weight)
        + product_right(value_low, value_weight)
    )
    return (
        share,
        spread,
        (query_low, key_low, value_low),
        query_sum[0],
        value_sum[0],
        jnp.sum(incoming, axis=0),
        table_grad,
    )


def mix(rows, gain, shift, pointwise_in, taps):
    normed, center, inverse = layer_norm(rows, gain, shift)
    normed = narrow(normed)
    linear = product(normed, pointwise_in[0])
    gate = product(normed, pointwise_in[1])
    mixed, sums = yield Met(mix_channels(linear, gate, taps))
    return mixed, wide_sum(sums), (rows, center, inverse, normed, linear, gate)


def convolve(mixed, sums, depth_gain, depth_shift, pointwise_out):
    center = (sums[0] / D)[:, None]
    channel_inverse = lax.rsqrt(sums[1][:, None] / D - center * center + epsilon)
    channel_normal = (mixed - center) * channel_inverse
    shaped = channel_normal * depth_gain + depth_shift
    active = narrow(shaped * jax.nn.sigmoid(shaped))
    return product(active, pointwise_out), (channel_inverse, channel_normal, shaped, active)


def shape_back(incoming, shape_kept, depth_gain, pointwise_out):
    channel_inverse, channel_normal, shaped, active = shape_kept
    spread = narrow(incoming)
    sigma = jax.nn.sigmoid(shaped)
    shaped_grad = product_right(spread, pointwise_out) * sigma * (1.0 + shaped * (1.0 - sigma))
    scaled = shaped_grad * depth_gain
    sums = wide_sum(
        jnp.stack([jnp.sum(scaled, axis=-1), jnp.sum(scaled * channel_normal, axis=-1)])
    )
    return (
        spread,
        scaled,
        sums,
        jnp.sum(shaped_grad * channel_normal, axis=0),
        jnp.sum(shaped_grad, axis=0),
    )


def convolve_back(scaled, sums, kept, shape_kept, pointwise_in, taps):
    linear, gate = kept[4:6]
    channel_inverse, channel_normal = shape_kept[:2]
    mixed_grad = channel_inverse * (
        scaled - (sums[0] / D)[:, None] - channel_normal * (sums[1] / D)[:, None]
    )
    linear_low, gating_low, taps_grad = mix_channels_back(mixed_grad, linear, gate, taps)
    share = product_right(linear_low, pointwise_in[0]) + product_right(gating_low, pointwise_in[1])
    return share, linear_low, gating_low, taps_grad[:CONV_K]


def total(parts):
    result = parts[0]
    for part in parts[1:]:
        result = result + part
    return result


def weight_grad_kernel(count, *refs):
    total = product_left(refs[0][...], refs[1][...])
    for place in range(1, count):
        total = total + product_left(refs[2 * place][...], refs[2 * place + 1][...])
    refs[2 * count][...] = narrow(total)


def tile_of(size, limit):
    tile = size
    while tile > limit:
        tile //= 2
    return tile


def weight_grad(lefts, rights):
    length, rows = lefts[0].shape
    columns = rights[0].shape[1]
    row_tile, column_tile = tile_of(rows, 1024), tile_of(columns, 1024)
    operands = [value for pair in zip(lefts, rights) for value in pair]
    return pl.pallas_call(
        functools.partial(weight_grad_kernel, len(lefts)),
        out_shape=jax.ShapeDtypeStruct((rows, columns), jnp.bfloat16),
        grid=(rows // row_tile, columns // column_tile),
        in_specs=[
            pl.BlockSpec((length, row_tile), lambda row, column: (0, row)),
            pl.BlockSpec((length, column_tile), lambda row, column: (0, column)),
        ]
        * len(lefts),
        out_specs=pl.BlockSpec((row_tile, column_tile), lambda row, column: (row, column)),
        compiler_params=pltpu.CompilerParams(vmem_limit_bytes=24 << 20),
        name="weight_grad",
    )(*operands)


class Gradients:
    def __init__(self, flow, count):
        self.flow = flow
        self.count = count
        self.parts = {}
        self.jobs = {}

    def add(self, name, part):
        parts = self.parts.setdefault(name, [])
        parts.append(part)
        return len(parts) == self.count

    def maker(self, name):
        parts = self.parts[name]
        return lambda: [
            weight_grad([part[place][0] for part in parts], [part[place][1] for part in parts])
            for place in range(len(parts[0]))
        ]

    def weights(self, name, pairs, width, delay=0, eager=False):
        if self.add(name, pairs):
            self.jobs[name] = self.flow.launch(scatter_job(self.maker(name), delay, width, eager))

    def sums(self, name, values):
        self.add(name, values)

    def reduce_sums(self, name, groups):
        values = []
        for group in groups:
            parts = self.parts[group]
            values.extend(total([part[place] for part in parts]) for place in range(len(parts[0])))
        self.jobs[name] = self.flow.launch(small_job(values))

    def whole(self, name, pairs):
        if self.add(name, pairs):
            self.jobs[name] = self.flow.launch(sum_job(self.maker(name)))

    def gather(self, name, members, turns=None):
        if members[-1] in self.jobs and name not in self.jobs:
            self.jobs[name] = self.flow.launch(
                gather_job([self.jobs[member] for member in members], turns)
            )

    def result(self, name):
        return self.jobs[name].result


def per_device(
    tokens,
    clip_count,
    first_norm_gain,
    first_norm_shift,
    first_up_weight,
    first_up_bias,
    first_down_weight,
    first_down_bias,
    attend_norm_gain,
    attend_norm_shift,
    query_weight,
    query_bias,
    key_weight,
    value_weight,
    value_bias,
    output_weight,
    output_bias,
    relative_table,
    convolve_norm_gain,
    convolve_norm_shift,
    pointwise_in,
    depthwise_weight,
    depth_norm_gain,
    depth_norm_shift,
    pointwise_out,
    second_norm_gain,
    second_norm_shift,
    second_up_weight,
    second_up_bias,
    second_down_weight,
    second_down_bias,
    final_norm_gain,
    final_norm_shift,
    cotangent,
):
    slots = range(tokens.shape[0])
    live_count = clip_count[0]
    first_gain = widen(first_norm_gain)
    attend_gain = widen(attend_norm_gain)
    convolve_gain = widen(convolve_norm_gain)
    second_gain = widen(second_norm_gain)
    final_gain = widen(final_norm_gain)
    taps = jnp.pad(widen(depthwise_weight), ((0, EDGE - CONV_K), (0, 0)))
    depth_gain = widen(depth_norm_gain)
    table, table_rows = table_forms(relative_table)
    flow = Flow()
    grads = Gradients(flow, len(slots))
    outputs = {}
    input_grads = {}
    count_job = flow.launch(small_job([jnp.full((1, 128), widen(live_count), jnp.float32)]))

    def clip(slot):
        live = (live_count > slot).astype(jnp.float32)
        rows = widen((yield Gathered(tokens[slot])))
        share, first_kept = feed_forward(
            rows,
            first_gain,
            widen(first_norm_shift),
            first_up_weight,
            widen(first_up_bias),
            first_down_weight,
        )
        rows = rows + 0.5 * ((yield Summed(share)) + widen(first_down_bias))
        share, attend_kept = attend(
            rows,
            attend_gain,
            widen(attend_norm_shift),
            query_weight,
            widen(query_bias),
            key_weight,
            value_weight,
            widen(value_bias),
            output_weight,
            table,
        )
        rows = rows + (yield Summed(share)) + widen(output_bias)
        mixed, sums, convolve_kept = yield from mix(
            rows, convolve_gain, widen(convolve_norm_shift), pointwise_in, taps
        )
        share, shape_kept = convolve(
            mixed, sums, depth_gain, widen(depth_norm_shift), pointwise_out
        )
        rows = rows + (yield Summed(share))
        share, second_kept = feed_forward(
            rows,
            second_gain,
            widen(second_norm_shift),
            second_up_weight,
            widen(second_up_bias),
            second_down_weight,
        )
        last = own_rows(rows) + 0.5 * ((yield Scattered(share)) + widen(second_down_bias))
        normed, center, inverse = layer_norm(last, final_gain, widen(final_norm_shift))
        outputs[slot] = narrow(normed * live)
        grad, gain_grad, shift_grad = norm_back(
            widen(cotangent[slot]) * live, (last - center) * inverse, inverse, final_gain
        )
        grads.sums("final", [gain_grad, shift_grad])

        grad = widen((yield Gathered(narrow(grad))))
        share, spread, before_low, up_sum, down_sum = feed_back(
            grad, second_kept, second_up_weight, second_down_weight
        )
        grads.whole("second_both", [(second_kept[5], spread), (second_kept[3], before_low)])
        normed_grad = yield Summed(share)
        grad, gain_grad, shift_grad = residual_back(grad, normed_grad, second_kept, second_gain)
        grads.sums("second", [up_sum, down_sum, gain_grad, shift_grad])

        spread, scaled, sums, depth_gain_sum, depth_shift_sum = shape_back(
            grad, shape_kept, depth_gain, pointwise_out
        )
        share, linear_low, gating_low, depthwise_sum = convolve_back(
            scaled, sums, convolve_kept, shape_kept, pointwise_in, taps
        )
        grads.weights(
            "convolve",
            [
                (convolve_kept[3], linear_low),
                (convolve_kept[3], gating_low),
                (shape_kept[3], spread),
            ],
            linear_low.shape[1],
        )
        normed_grad = yield Summed(share)
        grad, gain_grad, shift_grad = residual_back(
            grad, normed_grad, convolve_kept, convolve_gain
        )
        grads.sums(
            "convolve_sums", [depth_gain_sum, depth_shift_sum, depthwise_sum, gain_grad, shift_grad]
        )

        share, spread, lows, query_sum, value_sum, output_sum, table_sum = yield from attend_back(
            grad,
            attend_kept,
            query_weight,
            key_weight,
            value_weight,
            output_weight,
            table,
            table_rows,
        )
        grads.weights(
            "attend",
            [(attend_kept[7], spread)] + [(attend_kept[3], low) for low in lows],
            lows[0].shape[1],
            eager=True,
        )
        grads.sums("attend_sums", [query_sum, value_sum, output_sum, table_sum])
        grads.gather("middle", ["convolve", "attend"])
        normed_grad = yield Summed(share)
        grad, gain_grad, shift_grad = residual_back(grad, normed_grad, attend_kept, attend_gain)
        grads.sums("attend_norm", [gain_grad, shift_grad])

        share, spread, before_low, up_sum, down_sum = feed_back(
            grad, first_kept, first_up_weight, first_down_weight
        )
        grads.weights("first_down", [(first_kept[5], spread)], spread.shape[1], eager=True)
        grads.weights("first_up", [(first_kept[3], before_low)], spread.shape[1], 0, eager=True)
        grads.gather("first_both", ["first_down", "first_up"])
        normed_grad = yield Scattered(share)
        input_grads[slot], gain_grad, shift_grad = residual_back(
            own_rows(grad),
            normed_grad,
            [own_rows(kept) for kept in first_kept[:3]],
            first_gain,
        )
        grads.sums("first", [up_sum, down_sum])
        grads.sums("first_norm", [gain_grad, shift_grad])

    flow.run([clip(slot) for slot in slots])
    own = [
        total([part[place] for part in grads.parts[group]])
        for group, place in (
            ("final", 0),
            ("final", 1),
            ("first_norm", 0),
            ("first_norm", 1),
            ("attend_sums", 3),
        )
    ]
    flat = wide_sum(jnp.concatenate([value.reshape(-1) for value in own]))
    shared = []
    for value in own:
        shared.append(flat[: value.size].reshape(value.shape))
        flat = flat[value.size :]
    grads.parts["final"] = [shared[:2]]
    grads.parts["first_norm"] = [shared[2:4]]
    grads.parts["attend_sums"] = [
        [total([part[place] for part in grads.parts["attend_sums"]]) for place in range(3)]
        + shared[4:]
    ]
    grads.reduce_sums(
        "sums",
        [
            "final",
            "second",
            "convolve_sums",
            "attend_sums",
            "attend_norm",
            "first",
            "first_norm",
        ],
    )
    flow.drain()

    clips = count_job.result[0][0, 0]
    early, late = grads.result("sums")[:15], grads.result("sums")[15:]
    second_down, second_up = grads.result("second_both")
    linear, gating, point_out, output_grad, query_grad, key_grad, value_grad = grads.result("middle")
    first_down, first_up = grads.result("first_both")
    table_grad = early[14].T[: relative_table.shape[0]]
    every = (
        late[4],
        late[5],
        first_up,
        late[2],
        first_down,
        late[3],
        late[0],
        late[1],
        query_grad,
        early[11],
        key_grad,
        value_grad,
        early[12],
        output_grad,
        early[13],
        table_grad,
        early[9],
        early[10],
        jnp.stack([linear, gating]),
        early[8],
        early[6],
        early[7],
        point_out,
        early[4],
        early[5],
        second_up,
        early[2],
        second_down,
        early[3],
        early[0],
        early[1],
    )
    return (
        jnp.stack([outputs[slot] for slot in slots]),
        jnp.stack([input_grads[slot] for slot in slots]),
    ) + tuple(widen(value) / clips for value in every)


def solution(mesh):
    placed = (
        P("dp", "tensor", None),
        P("dp"),
        P(),
        P(),
        P(None, "tensor"),
        P("tensor"),
        P("tensor", None),
        P(),
        P(),
        P(),
        P(None, "tensor"),
        P("tensor"),
        P(None, "tensor"),
        P(None, "tensor"),
        P("tensor"),
        P("tensor", None),
        P(),
        P(),
        P(),
        P(),
        P(None, None, "tensor"),
        P(None, "tensor"),
        P("tensor"),
        P("tensor"),
        P("tensor", None),
        P(),
        P(),
        P(None, "tensor"),
        P("tensor"),
        P("tensor", None),
        P(),
        P(),
        P(),
        P("dp", "tensor", None),
    )
    return jax.shard_map(
        per_device,
        mesh=mesh,
        in_specs=placed,
        out_specs=(
            P("dp", "tensor", None),
            P("dp", "tensor", None),
            P(),
            P(),
            P(None, "tensor"),
            P("tensor"),
            P("tensor", None),
            P(),
            P(),
            P(),
            P(None, "tensor"),
            P("tensor"),
            P(None, "tensor"),
            P(None, "tensor"),
            P("tensor"),
            P("tensor", None),
            P(),
            P(),
            P(),
            P(),
            P(None, None, "tensor"),
            P(None, "tensor"),
            P("tensor"),
            P("tensor"),
            P("tensor", None),
            P(),
            P(),
            P(None, "tensor"),
            P("tensor"),
            P("tensor", None),
            P(),
            P(),
            P(),
        ),
        check_vma=False,
    )
```
